512 devices in a mesh: enc: 8 (over x, core), row: 4 (over y_lo), col: 16 (over z, y_hi).
Axes of the slice: x: 4, y: 8 (y_hi: 2, y_lo: 4; y = y_hi * 4 + y_lo), z: 8, core: 2. Of those that a mesh axis runs over, the one named last changes fastest.
Arguments:
- queries: bfloat16 [10240, 3072], P(('row', 'col'), 'enc'), may hold values from -150 to 150
- self_keys: bfloat16 [10240, 3072], P(('row', 'col'), 'enc'), may hold values from -150 to 150
- self_values: bfloat16 [10240, 3072], P(('row', 'col'), 'enc'), may hold values from -6 to 6
- positions: int32 [10240, 3], P(('row', 'col')), may hold values from 0 to 63, as said below
- query_gain: float32 [3072], P('enc'), may hold values from 1.3 to 2
- key_gain: float32 [3072], P('enc'), may hold values from 1.3 to 2
- context_keys: bfloat16 [128, 3072], P(('enc', 'row')), may hold values from -150 to 150
- context_values: bfloat16 [128, 3072], P(('enc', 'row')), may hold values from -6 to 6
- context_gain: float32 [3072], replicated, may hold values from 0.1 to 1.9
- image_cotangent: bfloat16 [10240, 3072], P(('row', 'col'), 'enc'), may hold values from -6 to 6
Outputs:
- self_mixed: bfloat16 [10240, 3072], P(('row', 'col'), 'enc')
- image_mixed: bfloat16 [10240, 3072], P(('row', 'col'), 'enc')
- grad_context_keys: float32 [128, 3072], P(('enc', 'row'))
- grad_context_values: float32 [128, 3072], P(('enc', 'row'))
The draws below stay inside these ranges and needn't reach their ends.
Inputs may be any that keep to these rules, and one draw needn't show every extreme that they name: `positions`: each (frame, patch row, patch column) of the 5 x 32 x 64 grid appears once; the tokens of one device form one tile of 8 x 4 patches in every frame, in order of frame, row, column; which tile lies on which device is drawn.
All inputs are finite; a program needn't handle non-finite values.
Results may differ from the reference program's by a relative error of at most 0.002.
The reference program's roundings to bfloat16 on the way (of `query_turned`, `key_turned`, `weights`, `query_plain`, `context_normed`, `probs_low` and `grad_scores`) count: a program that leaves them out, or rounds other values in their place, can miss the bound.
Values may be sent and summed in bfloat16 or wider, within the bound.
A program may use at most 128 MiB of HBM per device.

```python
import math
import jax
import jax.numpy as jnp
from jax import lax

HEADS = 24
HEAD_DIM = 128
TILE_H = 8
TILE_W = 4
WIDTH = 3072
GH = 32
GW = 64
TILE = 160
TOKENS = 10240
CTX = 128


def feature_scales(key, falling):
    head_rank = (jnp.arange(WIDTH) // HEAD_DIM).astype(jnp.float32)
    share = head_rank / max(HEADS - 1, 1)
    if falling:
        share = 1.0 - share
    ramped = 2.0 ** share
    rough = jnp.exp(jax.random.uniform(key, (WIDTH,)) * math.log(10.0))
    return ramped * rough


def rough_rows(key, row_count, falling):
    base = jax.random.normal(jax.random.fold_in(key, 1), (row_count, WIDTH))
    row_scale = jnp.exp(jax.random.uniform(jax.random.fold_in(key, 2), (row_count, 1)) * math.log(10.0))
    return base * row_scale * feature_scales(jax.random.fold_in(key, 3), falling) / 10.0


def draw_queries(key, part):
    drawn = rough_rows(jax.random.fold_in(key, 101), TOKENS, False)
    return jnp.clip(drawn, -150.0, 150.0).astype(jnp.bfloat16)


def draw_self_keys(key, part):
    drawn = rough_rows(jax.random.fold_in(key, 202), TOKENS, True)
    return jnp.clip(drawn, -150.0, 150.0).astype(jnp.bfloat16)


def draw_context_keys(key, part):
    drawn = rough_rows(jax.random.fold_in(key, 303), CTX, False)
    return jnp.clip(drawn, -150.0, 150.0).astype(jnp.bfloat16)


def draw_positions(key, part):
    tiles_down = GH // TILE_H
    tiles_across = GW // TILE_W
    tile_count = tiles_down * tiles_across
    order = jax.random.permutation(jax.random.fold_in(key, 7), tile_count)
    local = jnp.arange(TILE)
    frame = local // (TILE_H * TILE_W)
    down = local // TILE_W % TILE_H
    across = local % TILE_W
    tile_row = order // tiles_across
    tile_col = order % tiles_across
    coords = jnp.stack([jnp.broadcast_to(frame[None, :], (tile_count, TILE)), tile_row[:, None] * TILE_H + down[None, :], tile_col[:, None] * TILE_W + across[None, :]], axis=-1)
    return coords.reshape(TOKENS, 3).astype(jnp.int32)


def level_of(rng, shape, split, low, top_value):
    factor_of = 1.0
    for dim, shards_of in split:
        heights = jax.random.uniform(jax.random.fold_in(jax.random.fold_in(rng, 6), dim), (shards_of,), jnp.float32, low / len(split), top_value / len(split))
        factor_of = factor_of * jnp.repeat(jnp.exp(heights), shape[dim] // shards_of).reshape((-1,) + (1,) * (len(shape) - 1 - dim))
    return factor_of


def centred(own_key, extent, width, reach, split=(), held_as=jnp.bfloat16):
    level = level_of(own_key, extent, split, -0.22, 0.18) if split else 1.0
    array = jax.random.normal(own_key, extent, jnp.float32) * width * level
    return jnp.minimum(jnp.maximum(array, -reach), reach).astype(held_as)


def setup_inputs(seed: int = 0) -> dict:
    key_of = jax.random.split(jax.random.key(seed), 11)
    queries = draw_queries(jax.random.fold_in(key_of[10], 71), 0)
    self_keys = draw_self_keys(jax.random.fold_in(key_of[10], 71), 0)
    self_values = centred(key_of[2], (TOKENS, WIDTH), 1.0, 6.0, ((0, 64), (1, 8)))
    positions = draw_positions(jax.random.fold_in(key_of[10], 71), 0)
    query_gain = jnp.clip(jnp.exp(math.log(2.0) - 0.43078295 * jax.random.uniform(key_of[4], (WIDTH,), jnp.float32) ** level_of(key_of[4], (WIDTH,), ((0, 8),), -0.2, 0.2)), 1.3, 2.0)
    key_gain = jnp.clip(jnp.exp(math.log(2.0) - 0.43078295 * jax.random.uniform(key_of[5], (WIDTH,), jnp.float32) ** level_of(key_of[5], (WIDTH,), ((0, 8),), -0.2, 0.2)), 1.3, 2.0)
    context_keys = draw_context_keys(jax.random.fold_in(key_of[10], 71), 0)
    context_values = centred(key_of[7], (CTX, WIDTH), 1.0, 6.0, ((0, 32),))
    context_gain = jnp.clip(1.0 + 0.18 * jax.random.normal(key_of[8], (WIDTH,), jnp.float32), 0.1, 1.9)
    image_cotangent = centred(key_of[9], (TOKENS, WIDTH), 1.0, 6.0, ((0, 64), (1, 8)))
    return dict(queries=queries, self_keys=self_keys, self_values=self_values, positions=positions, query_gain=query_gain, key_gain=key_gain, context_keys=context_keys, context_values=context_values, context_gain=context_gain, image_cotangent=image_cotangent)


eps = 1e-06

def rope_angles(positions):
    half = HEAD_DIM // 2
    part_side = HEAD_DIM // 6
    part_time = half - 2 * part_side
    freq_time = 1.0 / 10000.0 ** (jnp.arange(part_time, dtype=jnp.float32) * 2.0 / (2 * part_time))
    freq_side = 1.0 / 10000.0 ** (jnp.arange(part_side, dtype=jnp.float32) * 2.0 / (2 * part_side))
    zeros_side = jnp.zeros((part_side,), jnp.float32)
    zeros_time = jnp.zeros((part_time,), jnp.float32)
    time_row = jnp.concatenate([freq_time, zeros_side, zeros_side])
    height_row = jnp.concatenate([zeros_time, freq_side, zeros_side])
    width_row = jnp.concatenate([zeros_time, zeros_side, freq_side])
    coords = positions.astype(jnp.float32)
    return coords[:, 0:1] * time_row + coords[:, 1:2] * height_row + coords[:, 2:3] * width_row

def rms_normed(wide, gain):
    return wide * lax.rsqrt(lax.optimization_barrier(jnp.mean(wide * wide, axis=1, keepdims=True)) + eps) * gain

def rotate(normed, angles):
    row_count = normed.shape[0]
    half = HEAD_DIM // 2
    pairs = normed.reshape(row_count, HEADS, half, 2)
    even_part = pairs[..., 0]
    odd_part = pairs[..., 1]
    cosine = jnp.cos(angles)[:, None, :]
    sine = jnp.sin(angles)[:, None, :]
    turned = jnp.stack([even_part * cosine - odd_part * sine, even_part * sine + odd_part * cosine], axis=-1)
    return turned.reshape(row_count, HEADS * HEAD_DIM)

def rounded(wide):
    return lax.optimization_barrier(wide.astype(jnp.bfloat16)).astype(jnp.float32)

def by_heads(matrix, row_count):
    return matrix.reshape(row_count, HEADS, HEAD_DIM).transpose(1, 0, 2).astype(jnp.float32)

def self_attention(query_turned, key_turned, self_values, score_scale):
    block = math.gcd(TOKENS, 512)
    query_heads = by_heads(query_turned, TOKENS)
    key_heads = by_heads(key_turned, TOKENS)
    value_heads = by_heads(self_values, TOKENS)

    def one_head(operands):
        query_head, key_head, value_head = operands

        def one_block(query_block):
            scores = jnp.dot(query_block, key_head.T, precision=lax.Precision.HIGHEST) * score_scale
            peak = lax.optimization_barrier(jnp.max(scores, axis=1, keepdims=True))
            weights = jnp.exp(scores - peak)
            weight_sum = lax.optimization_barrier(jnp.sum(weights, axis=1, keepdims=True))
            mixed = jnp.dot(rounded(weights), value_head, precision=lax.Precision.HIGHEST)
            return mixed / weight_sum
        outcome = lax.map(one_block, query_head.reshape(TOKENS // block, block, HEAD_DIM))
        return outcome.reshape(TOKENS, HEAD_DIM)
    mixed = lax.map(one_head, (query_heads, key_heads, value_heads))
    return mixed.transpose(1, 0, 2).reshape(TOKENS, HEADS * HEAD_DIM).astype(jnp.bfloat16)

def cross_attention(query_plain, context_normed, context_values, image_cotangent, score_scale):
    query_heads = by_heads(query_plain, TOKENS)
    key_heads = by_heads(context_normed, CTX)
    value_heads = by_heads(context_values, CTX)
    cotangent_heads = by_heads(image_cotangent, TOKENS)

    def one_head(operands):
        query_head, key_head, value_head, cotangent_head = operands
        scores = jnp.dot(query_head, key_head.T, precision=lax.Precision.HIGHEST) * score_scale
        peak = lax.optimization_barrier(jnp.max(scores, axis=1, keepdims=True))
        weights = jnp.exp(scores - peak)
        probs = weights / lax.optimization_barrier(jnp.sum(weights, axis=1, keepdims=True))
        probs_low = rounded(probs)
        mixed = jnp.dot(probs_low, value_head, precision=lax.Precision.HIGHEST)
        grad_values = jnp.dot(probs_low.T, cotangent_head, precision=lax.Precision.HIGHEST)
        grad_probs = jnp.dot(cotangent_head, value_head.T, precision=lax.Precision.HIGHEST)
        inner = lax.optimization_barrier(jnp.sum(probs * grad_probs, axis=1, keepdims=True))
        grad_scores = rounded(probs * (grad_probs - inner))
        grad_keys = jnp.dot(grad_scores.T, query_head, precision=lax.Precision.HIGHEST) * score_scale
        return (mixed, grad_keys, grad_values)
    mixed, grad_keys, grad_values = lax.map(one_head, (query_heads, key_heads, value_heads, cotangent_heads))
    image_out = mixed.transpose(1, 0, 2).reshape(TOKENS, HEADS * HEAD_DIM).astype(jnp.bfloat16)
    grad_keys = grad_keys.transpose(1, 0, 2).reshape(CTX, HEADS * HEAD_DIM)
    grad_values = grad_values.transpose(1, 0, 2).reshape(CTX, HEADS * HEAD_DIM)
    return (image_out, grad_keys, grad_values)

def reference(queries, self_keys, self_values, positions, query_gain, key_gain, context_keys, context_values, context_gain, image_cotangent):
    score_scale = HEAD_DIM ** (-0.5)
    query_normed = rms_normed(queries.astype(jnp.float32), query_gain)
    key_normed = rms_normed(self_keys.astype(jnp.float32), key_gain)
    angles = rope_angles(positions)
    query_turned = rotate(query_normed, angles).astype(jnp.bfloat16)
    key_turned = rotate(key_normed, angles).astype(jnp.bfloat16)
    self_out = self_attention(query_turned, key_turned, self_values, score_scale)
    query_plain = query_normed.astype(jnp.bfloat16)
    context_wide = context_keys.astype(jnp.float32)
    context_recip = lax.rsqrt(lax.optimization_barrier(jnp.mean(context_wide * context_wide, axis=1, keepdims=True)) + eps)
    context_normed = (context_wide * context_recip * context_gain).astype(jnp.bfloat16)
    image_out, grad_normed, grad_values = cross_attention(query_plain, context_normed, context_values, image_cotangent, score_scale)
    scaled_grad = context_gain * grad_normed
    grad_keys = context_recip * scaled_grad - context_wide * context_recip ** 3 * lax.optimization_barrier(jnp.mean(context_wide * scaled_grad, axis=1, keepdims=True))
    return (self_out, image_out, grad_keys, grad_values)
```

```python
import functools
import math
import jax
import jax.numpy as jnp
import numpy as np
from jax import lax
from jax.experimental import pallas as pl
from jax.experimental.pallas import tpu as pltpu
from jax.sharding import PartitionSpec as P

D = 128
EPS = 1e-06
MESH = pl.DeviceIdType.MESH
f32 = jnp.float32
bf16 = jnp.bfloat16
NEG = -1e30
NT = (((1,), (1,)), ((), ()))
NN = (((1,), (0,)), ((), ()))
TN = (((0,), (0,)), ((), ()))


def dot(a, b, dims):
    return lax.dot_general(a, b, dims, preferred_element_type=f32)


def freq_rows():
    half = D // 2
    side = D // 6
    time = half - 2 * side
    ft = 1.0 / 10000.0 ** (np.arange(time, dtype=np.float32) * 2.0 / (2 * time))
    fs = 1.0 / 10000.0 ** (np.arange(side, dtype=np.float32) * 2.0 / (2 * side))
    rows = np.zeros((8, half), np.float32)
    rows[0, :time] = ft
    rows[1, time : time + side] = fs
    rows[2, time + side :] = fs
    return np.repeat(rows, 2, axis=1)


def kernel(
    cfg,
    q_ref, k_ref, v_ref, pos_ref, fr_ref, qg_ref, kg_ref, ck_ref, cv_ref, cg_ref, cot_ref,
    so_ref, io_ref, gk_ref, gv_ref,
    Q, K, V, S, O, OR, X1s, X1, X2, ST, MS, MR, LS, LR, G1s, G1, G2s, G2, G3, G4, qp,
    loc_sem, gs_sem, gr_sem, os_sem, or_sem, xs_sem, xr_sem,
):
    E, R, YH, N, T, W, H = cfg
    W2 = W * E
    scale = D ** -0.5
    e = lax.axis_index("enc")
    row = lax.axis_index("row")
    col = lax.axis_index("col")
    z = col // YH
    y = (col % YH) * R + row
    c = e % 2
    a = y * (1 - c) + z * c
    b = z * (1 - c) + y * c
    FW = N // 2
    BW = N - 1 - FW

    def dev(e_, y_, z_):
        return (e_, y_ % R, z_ * YH + y_ // R)

    def e_dev(d):
        return dev((e + d) % E, y, z)

    def y_dev(d):
        return dev(e, (y + d) % N, z)

    def z_dev(d):
        return dev(e, y, (z + d) % N)

    def a_dev(p):
        return dev(e, (1 - c) * p + c * y, (1 - c) * z + c * p)

    def b_dev(p):
        return dev(e, (1 - c) * y + c * p, (1 - c) * p + c * z)

    def row_dev(d):
        return (e, (row + d) % R, col)

    def remote(src, dst, ssem, rsem, device):
        return pltpu.make_async_remote_copy(
            src_ref=src, dst_ref=dst, send_sem=ssem, recv_sem=rsem,
            device_id=device, device_id_type=MESH,
        )

    bar = pltpu.get_barrier_semaphore()
    peers = [e_dev(d) for d in range(1, E)]
    peers += [y_dev(d) for d in range(1, N)] + [z_dev(d) for d in range(1, N)]
    for p in peers:
        pl.semaphore_signal(bar, inc=1, device_id=p, device_id_type=MESH)
    pl.semaphore_wait(bar, len(peers))

    def fwd_pos(p, s):
        return (p + (1 - 2 * c) * s + 2 * N) % N

    def ring(i, buf, p, who, fwd, s):
        sg = 1 if fwd else -1
        slot = fwd_pos(p, -sg * s)
        sl = buf.at[:, pl.ds(pl.multiple_of(slot * T, T), T), :]
        k_ = s if fwd else FW + s
        return remote(sl, sl, gs_sem.at[i, k_], gr_sem.at[i, k_], who(fwd_pos(p, sg)))

    rings = {"q": (0, Q, a, a_dev), "k": (1, K, b, b_dev), "v": (2, V, b, b_dev)}

    def ring_start(t, s):
        if s < FW:
            ring(*rings[t], True, s).start()
        if s < BW:
            ring(*rings[t], False, s).start()

    def ring_recv(t, s):
        if s < FW:
            ring(*rings[t], True, s).wait_recv()
        if s < BW:
            ring(*rings[t], False, s).wait_recv()

    def ring_sent(t):
        for s in range(FW):
            ring(*rings[t], True, s).wait_send()
        for s in range(BW):
            ring(*rings[t], False, s).wait_send()

    def ring_next(t, s):
        ring_recv(t, s - 1)
        if s < FW:
            ring_start(t, s)

    a0 = pl.multiple_of(a * T, T)
    b0 = pl.multiple_of(b * T, T)
    for h in range(H):
        pltpu.make_async_copy(
            v_ref.at[:, pl.ds(h * D, D)], V.at[h, pl.ds(b0, T), :], loc_sem.at[h]
        ).start()

    eye = lax.broadcasted_iota(jnp.int32, (T, T), 0) == lax.broadcasted_iota(jnp.int32, (T, T), 1)

    def to_row(colv):
        return jnp.sum(jnp.where(eye, jnp.broadcast_to(colv, (T, T)), 0.0), axis=0, keepdims=True)

    def to_col(rowv):
        return jnp.sum(jnp.where(eye, jnp.broadcast_to(rowv, (T, T)), 0.0), axis=1, keepdims=True)

    qw = q_ref[...].astype(f32)
    kw = k_ref[...].astype(f32)
    srow_q = to_row(jnp.sum(qw * qw, axis=1, keepdims=True))
    srow_k = to_row(jnp.sum(kw * kw, axis=1, keepdims=True))
    sub8 = lax.broadcasted_iota(jnp.int32, (8, T), 0)
    ST[e] = jnp.where(sub8 < 4, jnp.broadcast_to(srow_q, (8, T)), jnp.broadcast_to(srow_k, (8, T)))

    def xch(i, d, src, dst, device):
        return remote(src, dst, xs_sem.at[i, d], xr_sem.at[i, d], device)

    def st_x(d):
        return xch(0, d, ST.at[e], ST.at[e], e_dev(d))

    for d in range(1, E):
        st_x(d).start()

    for h in range(H):
        pltpu.make_async_copy(
            v_ref.at[:, pl.ds(h * D, D)], V.at[h, pl.ds(b0, T), :], loc_sem.at[h]
        ).wait()
    ring_start("v", 0)

    ckw = ck_ref[...].astype(f32)
    crecip = lax.rsqrt(jnp.mean(ckw * ckw, axis=1, keepdims=True) + EPS)
    cn = (ckw * crecip * cg_ref[...]).astype(bf16).astype(f32)
    cvw = cv_ref[...].astype(f32)
    for j in range(E):
        X1s[j, 0:4, :] = cn[:, j * W : (j + 1) * W]
        X1s[j, 4:8, :] = cvw[:, j * W : (j + 1) * W]

    def x1_x(d):
        return xch(1, d, X1s.at[(e + d) % E], X1.at[e], e_dev(d))

    for d in range(1, E):
        x1_x(d).start()
    X1[e] = X1s[e]

    coords = pos_ref[...].astype(f32)
    ang = (
        coords[:, 0:1] * fr_ref[0:1, :]
        + coords[:, 1:2] * fr_ref[1:2, :]
        + coords[:, 2:3] * fr_ref[2:3, :]
    )
    lane = lax.broadcasted_iota(jnp.int32, (T, D), 1)
    even = lane % 2 == 0
    cosv = jnp.cos(ang)
    sinv = jnp.sin(ang)
    sinv = jnp.where(even, -sinv, sinv)

    for d in range(1, E):
        st_x(d).wait_recv()
    tot = ST[0]
    for j in range(1, E):
        tot = tot + ST[j]
    qn = qw * lax.rsqrt(to_col(tot[0:1, :]) / W2 + EPS) * qg_ref[...]
    kn = kw * lax.rsqrt(to_col(tot[4:5, :]) / W2 + EPS) * kg_ref[...]
    qp[...] = qn.astype(bf16)

    def turn(x):
        swapped = jnp.where(even, pltpu.roll(x, D - 1, 1), pltpu.roll(x, 1, 1))
        return (x * cosv + swapped * sinv).astype(bf16)

    for h in range(H):
        Q[h, pl.ds(a0, T), :] = turn(qn[:, h * D : (h + 1) * D])
        K[h, pl.ds(b0, T), :] = turn(kn[:, h * D : (h + 1) * D])
    ring_start("q", 0)
    ring_start("k", 0)

    for d in range(1, E):
        x1_x(d).wait_recv()
    X2[row] = X1[...].reshape(E * 8, W).astype(bf16)

    def x2_x(d):
        return xch(2, d, X2.at[row], X2.at[row], row_dev(d))

    for d in range(1, R):
        x2_x(d).start()
    ring_next("v", 1)
    ring_next("q", 1)
    ring_next("k", 1)
    for d in range(1, R):
        x2_x(d).wait_recv()

    C2 = R * E * 8
    xall = X2[...].reshape(C2, W)
    xval = pltpu.roll(xall.astype(f32), C2 - 4, 0).astype(bf16)
    is_key_l = lax.broadcasted_iota(jnp.int32, (T, C2), 1) % 8 < 4
    is_key_s = lax.broadcasted_iota(jnp.int32, (C2, D), 0) % 8 < 4

    def image_head(h):
        hs = slice(h * D, (h + 1) * D)
        qh = qp[:, hs]
        th = cot_ref[:, hs]
        sc = dot(qh, xall[:, hs], NT) * scale
        sc = jnp.where(is_key_l, sc, NEG)
        w = jnp.exp(sc - jnp.max(sc, axis=1, keepdims=True))
        pr = w / jnp.sum(w, axis=1, keepdims=True)
        plo = pr.astype(bf16)
        io_ref[:, hs] = dot(plo, xval[:, hs], NN).astype(bf16)
        gv = dot(plo, th, TN)
        gp = dot(th, xval[:, hs], NT)
        inner = jnp.sum(pr * gp, axis=1, keepdims=True)
        gsc = (pr * (gp - inner)).astype(bf16)
        gk = dot(gsc, qh, TN) * scale
        both = jnp.where(is_key_s, gk, pltpu.roll(gv, 4, 0))
        for r in range(R):
            for j in range(E):
                lo = (r * E + j) * 8
                G1s[j, r, :, hs] = both[lo : lo + 8, :]

    for s in range(2, FW + 1):
        if s - 2 < H:
            image_head(s - 2)
        for t in ("v", "q", "k"):
            ring_next(t, s)
    for h in range(FW - 1, H):
        image_head(h)

    def g1_x(d):
        j = (z + d) % N
        return xch(3, d, G1s.at[j], G1.at[z], z_dev(d))

    for d in range(1, N):
        g1_x(d).start()
    G1[z] = G1s[z]

    def pass1(h):
        def body(i, carry):
            rows = pl.ds(pl.multiple_of(i * T, T), T)
            s = dot(Q[h, rows, :], K[h], NT)
            S[h, rows, :] = s
            MS[h, pl.ds(i, 1), :] = to_row(jnp.max(s, axis=1, keepdims=True))
            return carry

        lax.fori_loop(0, N, body, 0)

    def m_x(h, d):
        return xch(6 + h, d, MS.at[h], MR.at[h, a], a_dev((a + d) % N))

    def send_max(h):
        for d in range(1, N):
            m_x(h, d).start()
        MR[h, a] = MS[h]

    for h in range(H):
        pass1(h)
        send_max(h)
        if h == min(1, H - 1):
            for d in range(1, N):
                g1_x(d).wait_recv()
            g = G1[0]
            for j in range(1, N):
                g = g + G1[j]
            G2s[...] = g

            def g2_x(d):
                return xch(4, d, G2s.at[(y + d) % N % R], G2.at[y], y_dev(d))

            for d in range(1, N):
                g2_x(d).start()
            G2[y] = G2s[row]

    def pass2(h):
        for d in range(1, N):
            m_x(h, d).wait_recv()
        gm = MR[h, 0]
        for j in range(1, N):
            gm = jnp.maximum(gm, MR[h, j])
        MS[H] = gm

        def body(i, carry):
            rows = pl.ds(pl.multiple_of(i * T, T), T)
            mc = to_col(MS[H, pl.ds(i, 1), :])
            w = jnp.exp2((S[h, rows, :] - mc) * (scale * math.log2(math.e)))
            LS[i, h : h + 1, :] = to_row(jnp.sum(w, axis=1, keepdims=True))
            O[h, i] = dot(w.astype(bf16), V[h], NN)
            return carry

        lax.fori_loop(0, N, body, 0)

    def o_x(h, d):
        p = (a + d) % N
        return remote(
            O.at[h, p], OR.at[h, d], os_sem.at[h, d], or_sem.at[h, d], a_dev(p)
        )

    def l_x(d):
        p = (a + d) % N
        return xch(5, d, LS.at[p], LR.at[a], a_dev(p))

    for h in range(H):
        pass2(h)
        for d in range(1, N):
            o_x(h, d).start()
        if h == 0:
            for d in range(1, N):
                g2_x(d).wait_recv()
            g = G2[0]
            for j in range(1, N):
                g = g + G2[j]
            G3[z] = g

            def g3_x(d):
                return xch(6 + H, d, G3.at[z], G3.at[z], z_dev(d))

            for d in range(1, N):
                g3_x(d).start()
    for d in range(1, N):
        l_x(d).start()
    LR[a] = LS[a]

    for d in range(1, N):
        g3_x(d).wait_recv()

    def g4_x(d):
        return xch(7 + H, d, G3.at[(e + d) % E], G4.at[e], e_dev(d))

    for d in range(1, E):
        g4_x(d).start()
    G4[e] = G3[e]

    for d in range(1, N):
        l_x(d).wait_recv()
    lt = LR[0]
    for j in range(1, N):
        lt = lt + LR[j]

    for d in range(1, E):
        g4_x(d).wait_recv()
    for j in range(E):
        js = slice(j * W, (j + 1) * W)
        gv_ref[:, js] = G4[j, 4:8, :]
        gk_ref[:, js] = G4[j, 0:4, :]
    sg = cg_ref[...] * gk_ref[...]
    gk_ref[...] = crecip * sg - ckw * (crecip * crecip * crecip) * jnp.mean(
        ckw * sg, axis=1, keepdims=True
    )

    for h in range(H):
        acc = O[h, a]
        for d in range(1, N):
            o_x(h, d).wait_recv()
            acc = acc + OR[h, d]
        so_ref[:, h * D : (h + 1) * D] = (acc / to_col(lt[h : h + 1, :])).astype(bf16)

    for t in ("q", "k", "v"):
        ring_sent(t)
    for d in range(1, E):
        st_x(d).wait_send()
        x1_x(d).wait_send()
        g4_x(d).wait_send()
    for d in range(1, R):
        x2_x(d).wait_send()
    for d in range(1, N):
        g1_x(d).wait_send()
        g2_x(d).wait_send()
        g3_x(d).wait_send()
        l_x(d).wait_send()
        for h in range(H):
            m_x(h, d).wait_send()
            o_x(h, d).wait_send()


def per_device(mesh_shape, q, k, v, pos, qg, kg, ck, cv, cg, cot):
    E, R, CL = mesh_shape
    T, W = q.shape
    H = W // D
    N = int(math.isqrt(R * CL))
    YH = N // R
    cfg = (E, R, YH, N, T, W, H)
    vm = pl.BlockSpec(memory_space=pltpu.VMEM)
    dma = pltpu.SemaphoreType.DMA
    out_shape = (
        jax.ShapeDtypeStruct((T, W), bf16),
        jax.ShapeDtypeStruct((T, W), bf16),
        jax.ShapeDtypeStruct(ck.shape, f32),
        jax.ShapeDtypeStruct(ck.shape, f32),
    )
    MX = max(E, N)
    scratch = [
        pltpu.VMEM((H, N * T, D), bf16),
        pltpu.VMEM((H, N * T, D), bf16),
        pltpu.VMEM((H, N * T, D), bf16),
        pltpu.VMEM((H, N * T, N * T), f32),
        pltpu.VMEM((H, N, T, D), f32),
        pltpu.VMEM((H, N, T, D), f32),
        pltpu.VMEM((E, 8, W), f32),
        pltpu.VMEM((E, 8, W), f32),
        pltpu.VMEM((R, E * 8, W), bf16),
        pltpu.VMEM((E, 8, T), f32),
        pltpu.VMEM((H + 1, N, T), f32),
        pltpu.VMEM((H, N, N, T), f32),
        pltpu.VMEM((N, 8, T), f32),
        pltpu.VMEM((N, 8, T), f32),
        pltpu.VMEM((N, R, 8, W), f32),
        pltpu.VMEM((N, R, 8, W), f32),
        pltpu.VMEM((R, 8, W), f32),
        pltpu.VMEM((N, 8, W), f32),
        pltpu.VMEM((N, 8, W), f32),
        pltpu.VMEM((E, 8, W), f32),
        pltpu.VMEM((T, W), bf16),
        dma((H,)),
        dma((3, N)),
        dma((3, N)),
        dma((H, N)),
        dma((H, N)),
        dma((8 + H, MX)),
        dma((8 + H, MX)),
    ]
    return pl.pallas_call(
        functools.partial(kernel, cfg),
        out_shape=out_shape,
        in_specs=[vm] * 11,
        out_specs=(vm,) * 4,
        scratch_shapes=scratch,
        compiler_params=pltpu.CompilerParams(
            collective_id=0, has_side_effects=True, vmem_limit_bytes=56 * 2**20
        ),
    )(q, k, v, pos, jnp.asarray(freq_rows()), qg[None, :], kg[None, :], ck, cv, cg[None, :], cot)


def solution(mesh):
    shape = (mesh.shape["enc"], mesh.shape["row"], mesh.shape["col"])
    tok = P(("row", "col"), "enc")
    ctx = P(("enc", "row"), None)
    return jax.shard_map(
        functools.partial(per_device, shape),
        mesh=mesh,
        in_specs=(tok, tok, tok, P(("row", "col"), None), P("enc"), P("enc"), ctx, ctx, P(), tok),
        out_specs=(tok, tok, ctx, ctx),
        check_vma=False,
    )
```

```python
import functools
import math
import jax
import jax.numpy as jnp
import numpy as np
from jax import lax
from jax.experimental import pallas as pl
from jax.experimental.pallas import tpu as pltpu
from jax.sharding import PartitionSpec as P

D = 128
EPS = 1e-06
MESH = pl.DeviceIdType.MESH
f32 = jnp.float32
bf16 = jnp.bfloat16
NEG = -1e30
NT = (((1,), (1,)), ((), ()))
NN = (((1,), (0,)), ((), ()))
TN = (((0,), (0,)), ((), ()))


def dot(a, b, dims):
    return lax.dot_general(a, b, dims, preferred_element_type=f32)


def freq_rows():
    half = D // 2
    side = D // 6
    time = half - 2 * side
    ft = 1.0 / 10000.0 ** (np.arange(time, dtype=np.float32) * 2.0 / (2 * time))
    fs = 1.0 / 10000.0 ** (np.arange(side, dtype=np.float32) * 2.0 / (2 * side))
    rows = np.zeros((8, half), np.float32)
    rows[0, :time] = ft
    rows[1, time : time + side] = fs
    rows[2, time + side :] = fs
    return np.repeat(rows, 2, axis=1)


def kernel(
    cfg,
    q_ref, k_ref, v_ref, pos_ref, fr_ref, qg_ref, kg_ref, ck_ref, cv_ref, cg_ref, cot_ref,
    so_ref, io_ref, gk_ref, gv_ref,
    Q, K, V, S, O, ORF, ORB, X1s, X1, X2, ST, MS, MR, LS, LR, G1s, G1, G2s, G2, G3, G4, qp,
    loc_sem, gs_sem, gr_sem, os_sem, or_sem, xs_sem, xr_sem,
):
    E, R, YH, N, T, W, H = cfg
    W2 = W * E
    scale = D ** -0.5
    e = lax.axis_index("enc")
    row = lax.axis_index("row")
    col = lax.axis_index("col")
    z = col // YH
    y = (col % YH) * R + row
    c = e % 2
    a = y * (1 - c) + z * c
    b = z * (1 - c) + y * c
    FW = N // 2
    BW = N - 1 - FW

    def dev(e_, y_, z_):
        return (e_, y_ % R, z_ * YH + y_ // R)

    def e_dev(d):
        return dev((e + d) % E, y, z)

    def y_dev(d):
        return dev(e, (y + d) % N, z)

    def z_dev(d):
        return dev(e, y, (z + d) % N)

    def a_dev(p):
        return dev(e, (1 - c) * p + c * y, (1 - c) * z + c * p)

    def b_dev(p):
        return dev(e, (1 - c) * y + c * p, (1 - c) * p + c * z)

    def row_dev(d):
        return (e, (row + d) % R, col)

    def remote(src, dst, ssem, rsem, device):
        return pltpu.make_async_remote_copy(
            src_ref=src, dst_ref=dst, send_sem=ssem, recv_sem=rsem,
            device_id=device, device_id_type=MESH,
        )

    bar = pltpu.get_barrier_semaphore()
    peers = [e_dev(d) for d in range(1, E)]
    peers += [y_dev(d) for d in range(1, N)] + [z_dev(d) for d in range(1, N)]
    peers += [dev(z, y, (z + d) % N) for d in range(1, N)]
    peers += [dev((e + d) % E, y, e) for d in range(1, E)]
    for p in peers:
        pl.semaphore_signal(bar, inc=1, device_id=p, device_id_type=MESH)

    @pl.when(e != z)
    def _():
        for p in (dev(z, y, z), dev(e, y, e)):
            pl.semaphore_signal(bar, inc=1, device_id=p, device_id_type=MESH)

    BAR = len(peers) + jnp.where(e != z, 2, 0)

    def fwd_pos(p, s):
        return (p + (1 - 2 * c) * s + 2 * N) % N

    def ring(i, buf, p, who, h, fwd, s):
        sg = 1 if fwd else -1
        rows = pl.ds(pl.multiple_of(fwd_pos(p, -sg * s) * T, T), T)
        sl = buf.at[:, rows, :] if h is None else buf.at[h, rows, :]
        k_ = s if fwd else FW + s
        g = 0 if h is None else h
        return remote(
            sl, sl, gs_sem.at[i, g, k_], gr_sem.at[i, g, k_], who(fwd_pos(p, sg))
        )

    rings = {"q": (0, Q, a, a_dev), "k": (1, K, b, b_dev), "v": (2, V, b, b_dev)}

    def ring_start(t, h, s):
        if s < FW:
            ring(*rings[t], h, True, s).start()
        if s < BW:
            ring(*rings[t], h, False, s).start()

    def ring_recv(t, h, s):
        if s < FW:
            ring(*rings[t], h, True, s).wait_recv()
        if s < BW:
            ring(*rings[t], h, False, s).wait_recv()

    def ring_sent(t, h):
        for s in range(FW):
            ring(*rings[t], h, True, s).wait_send()
        for s in range(BW):
            ring(*rings[t], h, False, s).wait_send()

    def ring_next(t, h, s):
        if s >= FW:
            return
        ring_recv(t, h, s - 1)
        ring_start(t, h, s)

    a0 = pl.multiple_of(a * T, T)
    b0 = pl.multiple_of(b * T, T)
    for h in range(H):
        pltpu.make_async_copy(
            v_ref.at[:, pl.ds(h * D, D)], V.at[h, pl.ds(b0, T), :], loc_sem.at[h]
        ).start()

    eye = lax.broadcasted_iota(jnp.int32, (T, T), 0) == lax.broadcasted_iota(jnp.int32, (T, T), 1)

    def to_row(colv):
        return jnp.sum(jnp.where(eye, jnp.broadcast_to(colv, (T, T)), 0.0), axis=0, keepdims=True)

    def to_col(rowv):
        return jnp.sum(jnp.where(eye, jnp.broadcast_to(rowv, (T, T)), 0.0), axis=1, keepdims=True)

    qw = q_ref[...].astype(f32)
    kw = k_ref[...].astype(f32)
    srow_q = to_row(jnp.sum(qw * qw, axis=1, keepdims=True))
    srow_k = to_row(jnp.sum(kw * kw, axis=1, keepdims=True))
    sub8 = lax.broadcasted_iota(jnp.int32, (8, T), 0)
    ST[e] = jnp.where(sub8 < 4, jnp.broadcast_to(srow_q, (8, T)), jnp.broadcast_to(srow_k, (8, T)))

    def xch(i, d, src, dst, device):
        return remote(src, dst, xs_sem.at[i, d], xr_sem.at[i, d], device)

    def st_x(d):
        return xch(0, d, ST.at[e], ST.at[e], e_dev(d))

    pl.semaphore_wait(bar, BAR)
    for d in range(1, E):
        st_x(d).start()

    for h in range(H):
        pltpu.make_async_copy(
            v_ref.at[:, pl.ds(h * D, D)], V.at[h, pl.ds(b0, T), :], loc_sem.at[h]
        ).wait()
    ring_start("v", None, 0)

    ckw = ck_ref[...].astype(f32)
    crecip = lax.rsqrt(jnp.mean(ckw * ckw, axis=1, keepdims=True) + EPS)
    cn = (ckw * crecip * cg_ref[...].reshape(1, W2)).astype(bf16).astype(f32)
    cvw = cv_ref[...].astype(f32)
    for j in range(E):
        X1s[j, 0:4, :] = cn[:, j * W : (j + 1) * W]
        X1s[j, 4:8, :] = cvw[:, j * W : (j + 1) * W]

    def x1_x(d):
        return xch(1, d, X1s.at[(e + d) % E], X1.at[e], e_dev(d))

    for d in range(1, E):
        x1_x(d).start()
    X1[e] = X1s[e]

    coords = pos_ref[...].astype(f32)
    ang = (
        to_col(coords[0:1, :]) * fr_ref[0:1, :]
        + to_col(coords[1:2, :]) * fr_ref[1:2, :]
        + to_col(coords[2:3, :]) * fr_ref[2:3, :]
    )
    lane = lax.broadcasted_iota(jnp.int32, (T, D), 1)
    even = lane % 2 == 0
    cosv = jnp.cos(ang)
    sinv = jnp.sin(ang)
    sinv = jnp.where(even, -sinv, sinv)

    ring_next("v", None, 1)
    for d in range(1, E):
        st_x(d).wait_recv()
    tot = ST[0]
    for j in range(1, E):
        tot = tot + ST[j]
    qn = qw * lax.rsqrt(to_col(tot[0:1, :]) / W2 + EPS) * qg_ref[...].reshape(1, W)
    kn = kw * lax.rsqrt(to_col(tot[4:5, :]) / W2 + EPS) * kg_ref[...].reshape(1, W)
    qp[...] = qn.astype(bf16)

    def turn(x):
        swapped = jnp.where(even, pltpu.roll(x, D - 1, 1), pltpu.roll(x, 1, 1))
        return (x * cosv + swapped * sinv).astype(bf16)

    for h in range(H):
        Q[h, pl.ds(a0, T), :] = turn(qn[:, h * D : (h + 1) * D])
        ring_start("q", h, 0)
        K[h, pl.ds(b0, T), :] = turn(kn[:, h * D : (h + 1) * D])
        ring_start("k", h, 0)
    ring_next("v", None, 2)

    for d in range(1, E):
        x1_x(d).wait_recv()
    X2[row] = X1[...].reshape(E * 8, W).astype(bf16)

    sig = 1 - 2 * c
    offs = {1: [], 2: [1], 4: [1, -1, 2 * sig]}[R]

    def x2_x(d):
        return xch(2, d, X2.at[row], X2.at[row], y_dev(offs[d] + N))

    for d in range(len(offs)):
        x2_x(d).start()
    for s in range(1, FW):
        for h in range(H):
            ring_next("q", h, s)
            ring_next("k", h, s)
        if s + 2 < FW:
            ring_next("v", None, s + 2)
    for d in range(len(offs)):
        x2_x(d).wait_recv()

    C2 = R * E * 8
    xall = X2[...].reshape(C2, W)
    xval = pltpu.roll(xall.astype(f32), C2 - 4, 0).astype(bf16)
    is_key_l = lax.broadcasted_iota(jnp.int32, (T, C2), 1) % 8 < 4
    is_key_s = lax.broadcasted_iota(jnp.int32, (C2, D), 0) % 8 < 4

    def image_head(h):
        hs = slice(h * D, (h + 1) * D)
        qh = qp[:, hs]
        th = cot_ref[:, hs]
        sc = dot(qh, xall[:, hs], NT) * scale
        sc = jnp.where(is_key_l, sc, NEG)
        w = jnp.exp(sc - jnp.max(sc, axis=1, keepdims=True))
        pr = w / jnp.sum(w, axis=1, keepdims=True)
        plo = pr.astype(bf16)
        io_ref[:, hs] = dot(plo, xval[:, hs], NN).astype(bf16)
        gv = dot(plo, th, TN)
        gp = dot(th, xval[:, hs], NT)
        inner = jnp.sum(pr * gp, axis=1, keepdims=True)
        gsc = (pr * (gp - inner)).astype(bf16)
        gk = dot(gsc, qh, TN) * scale
        both = jnp.where(is_key_s, gk, pltpu.roll(gv, 4, 0))
        for r in range(R):
            for j in range(E):
                lo = (r * E + j) * 8
                G1s[j, r, :, hs] = both[lo : lo + 8, :]

    for h in range(H):
        image_head(h)

    def g1_x(d):
        j = (z + d) % N
        return xch(3, d, G1s.at[j], G1.at[z], z_dev(d))

    for d in range(1, N):
        g1_x(d).start()
    G1[z] = G1s[z]

    def pass1(h):
        def body(i, carry):
            rows = pl.ds(pl.multiple_of(i * T, T), T)
            s = dot(Q[h, rows, :], K[h], NT)
            S[h, rows, :] = s
            MS[h, pl.ds(i, 1), :] = to_row(jnp.max(s, axis=1, keepdims=True))
            return carry

        lax.fori_loop(0, N, body, 0)

    def m_x(h, d):
        return xch(6 + h, d, MS.at[h], MR.at[h, a], a_dev((a + d) % N))

    def send_max(h):
        for d in range(1, N):
            m_x(h, d).start()
        MR[h, a] = MS[h]

    for h in range(H):
        ring_recv("q", h, FW - 1)
        ring_recv("k", h, FW - 1)
        pass1(h)
        send_max(h)

    def of(h, s):
        t = fwd_pos(a, FW - s)
        return remote(
            O.at[h, t], ORF.at[h, s], os_sem.at[h, s], or_sem.at[h, s], a_dev(fwd_pos(a, 1))
        ), t

    def ob(h, s):
        t = fwd_pos(a, s - BW)
        return remote(
            O.at[h, t], ORB.at[h, s], os_sem.at[h, FW + s], or_sem.at[h, FW + s],
            a_dev(fwd_pos(a, -1)),
        ), t

    def o_step(h, s):
        if s < FW:
            of(h, s - 1)[0].wait_recv()
            cp, t = of(h, s)
            O[h, t] = O[h, t] + ORF[h, s - 1]
            cp.start()
        if s < BW:
            ob(h, s - 1)[0].wait_recv()
            cp, t = ob(h, s)
            O[h, t] = O[h, t] + ORB[h, s - 1]
            cp.start()

    def pass2(h):
        for d in range(1, N):
            m_x(h, d).wait_recv()
        gm = MR[h, 0]
        for j in range(1, N):
            gm = jnp.maximum(gm, MR[h, j])
        MS[H] = gm

        def body(k_, carry):
            i = fwd_pos(a, (2 * (k_ % 2) - 1) * (FW - (k_ + 1) // 2))
            rows = pl.ds(pl.multiple_of(i * T, T), T)
            mc = to_col(MS[H, pl.ds(i, 1), :])
            w = jnp.exp2((S[h, rows, :] - mc) * (scale * math.log2(math.e)))
            LS[i, h : h + 1, :] = to_row(jnp.sum(w, axis=1, keepdims=True))
            O[h, i] = dot(w.astype(bf16), V[h], NN)
            return carry

        body(0, 0)
        of(h, 0)[0].start()
        lax.fori_loop(1, 3, body, 0)
        ob(h, 0)[0].start()
        lax.fori_loop(3, N, body, 0)

    def l_x(d):
        p = (a + d) % N
        return xch(5, d, LS.at[p], LR.at[a], a_dev(p))

    def g2_x(d):
        return xch(4, d, G2s.at[(y + d) % N % R], G2.at[y], y_dev(d))

    def g3_x(d):
        i = 6 + H
        return remote(
            G3.at[0], G4.at[e], xs_sem.at[i, d], xr_sem.at[i, e], dev(z, y, (z + d) % N)
        )

    def g3_from(d):
        i, j = 6 + H, (e + d) % E
        return remote(G3.at[0], G4.at[j], xs_sem.at[i, d], xr_sem.at[i, j], dev(j, y, e))

    ring_recv("v", None, FW - 1)
    for h in range(H):
        pass2(h)
        for j in range(h, -1, -1):
            o_step(j, h - j + 1)
        if h == 0:
            for d in range(1, N):
                g1_x(d).wait_recv()
            g = G1[0]
            for j in range(1, N):
                g = g + G1[j]
            G2s[...] = g
            for d in range(1, N):
                g2_x(d).start()
            G2[y] = G2s[row]
    for d in range(1, N):
        l_x(d).start()
    LR[a] = LS[a]

    for d in range(1, N):
        g2_x(d).wait_recv()
    g = G2[0]
    for j in range(1, N):
        g = g + G2[j]
    G3[0] = g

    @pl.when(e != z)
    def _():
        g3_x(0).start()

    @pl.when(e == z)
    def _():
        G4[e] = g

    for d in range(1, N):
        g3_x(d).start()

    lt = None
    for k_ in range(H, H + FW):
        for j in range(H - 1, -1, -1):
            s_ = k_ - j
            if 1 <= s_ < FW and s_ >= H - j + 1 - 0:
                o_step(j, s_)

    for d in range(1, N):
        l_x(d).wait_recv()
    lt = LR[0]
    for j in range(1, N):
        lt = lt + LR[j]
    for h in range(H):
        of(h, FW - 1)[0].wait_recv()
        ob(h, BW - 1)[0].wait_recv()
        acc = O[h, a] + ORF[h, FW - 1] + ORB[h, BW - 1]
        so_ref[:, h * D : (h + 1) * D] = (acc / to_col(lt[h : h + 1, :])).astype(bf16)

    @pl.when(e != z)
    def _():
        g3_from(0).wait_recv()

    for d in range(1, E):
        g3_from(d).wait_recv()
    for j in range(E):
        js = slice(j * W, (j + 1) * W)
        gv_ref[:, js] = G4[j, 4:8, :]
        gk_ref[:, js] = G4[j, 0:4, :]
    sg = cg_ref[...].reshape(1, W2) * gk_ref[...]
    gk_ref[...] = crecip * sg - ckw * (crecip * crecip * crecip) * jnp.mean(
        ckw * sg, axis=1, keepdims=True
    )

    for h in range(H):
        ring_sent("q", h)
        ring_sent("k", h)
        for s in range(FW):
            of(h, s)[0].wait_send()
        for s in range(BW):
            ob(h, s)[0].wait_send()
    ring_sent("v", None)
    for d in range(1, E):
        st_x(d).wait_send()
        x1_x(d).wait_send()
    for d in range(len(offs)):
        x2_x(d).wait_send()

    @pl.when(e != z)
    def _():
        g3_x(0).wait_send()

    for d in range(1, N):
        g1_x(d).wait_send()
        g2_x(d).wait_send()
        g3_x(d).wait_send()
        l_x(d).wait_send()
        for h in range(H):
            m_x(h, d).wait_send()


def per_device(mesh_shape, q, k, v, pos, qg, kg, ck, cv, cg, cot):
    E, R, CL = mesh_shape
    T, W = q.shape
    H = W // D
    N = int(math.isqrt(R * CL))
    YH = N // R
    cfg = (E, R, YH, N, T, W, H)
    vm = pl.BlockSpec(memory_space=pltpu.VMEM)
    dma = pltpu.SemaphoreType.DMA
    out_shape = (
        jax.ShapeDtypeStruct((T, W), bf16),
        jax.ShapeDtypeStruct((T, W), bf16),
        jax.ShapeDtypeStruct(ck.shape, f32),
        jax.ShapeDtypeStruct(ck.shape, f32),
    )
    MX = max(E, N)
    scratch = [
        pltpu.VMEM((H, N * T, D), bf16),
        pltpu.VMEM((H, N * T, D), bf16),
        pltpu.VMEM((H, N * T, D), bf16),
        pltpu.VMEM((H, N * T, N * T), f32),
        pltpu.VMEM((H, N, T, D), f32),
        pltpu.VMEM((H, N // 2, T, D), f32),
        pltpu.VMEM((H, N // 2, T, D), f32),
        pltpu.VMEM((E, 8, W), f32),
        pltpu.VMEM((E, 8, W), f32),
        pltpu.VMEM((R, E * 8, W), bf16),
        pltpu.VMEM((E, 8, T), f32),
        pltpu.VMEM((H + 1, N, T), f32),
        pltpu.VMEM((H, N, N, T), f32),
        pltpu.VMEM((N, 8, T), f32),
        pltpu.VMEM((N, 8, T), f32),
        pltpu.VMEM((N, R, 8, W), f32),
        pltpu.VMEM((N, R, 8, W), f32),
        pltpu.VMEM((R, 8, W), f32),
        pltpu.VMEM((N, 8, W), f32),
        pltpu.VMEM((N, 8, W), f32),
        pltpu.VMEM((E, 8, W), f32),
        pltpu.VMEM((T, W), bf16),
        dma((H,)),
        dma((3, H, N)),
        dma((3, H, N)),
        dma((H, N)),
        dma((H, N)),
        dma((8 + H, MX)),
        dma((8 + H, MX)),
    ]
    return pl.pallas_call(
        functools.partial(kernel, cfg),
        out_shape=out_shape,
        in_specs=[vm] * 11,
        out_specs=(vm,) * 4,
        scratch_shapes=scratch,
        compiler_params=pltpu.CompilerParams(
            collective_id=0, has_side_effects=True, vmem_limit_bytes=56 * 2**20
        ),
    )(q, k, v, pos.T, jnp.asarray(freq_rows()), qg, kg, ck, cv, cg, cot)


def solution(mesh):
    shape = (mesh.shape["enc"], mesh.shape["row"], mesh.shape["col"])
    tok = P(("row", "col"), "enc")
    ctx = P(("enc", "row"), None)
    return jax.shard_map(
        functools.partial(per_device, shape),
        mesh=mesh,
        in_specs=(tok, tok, tok, P(("row", "col"), None), P("enc"), P("enc"), ctx, ctx, P(), tok),
        out_specs=(tok, tok, ctx, ctx),
        check_vma=False,
    )
```

```python
import functools
import math
import jax
import jax.numpy as jnp
import numpy as np
from jax import lax
from jax.experimental import pallas as pl
from jax.experimental.pallas import tpu as pltpu
from jax.sharding import PartitionSpec as P

D = 128
EPS = 1e-06
MESH = pl.DeviceIdType.MESH
f32 = jnp.float32
bf16 = jnp.bfloat16
NEG = -1e30
NT = (((1,), (1,)), ((), ()))
NN = (((1,), (0,)), ((), ()))
TN = (((0,), (0,)), ((), ()))


def dot(a, b, dims):
    return lax.dot_general(a, b, dims, preferred_element_type=f32)


def freq_rows():
    half = D // 2
    side = D // 6
    time = half - 2 * side
    ft = 1.0 / 10000.0 ** (np.arange(time, dtype=np.float32) * 2.0 / (2 * time))
    fs = 1.0 / 10000.0 ** (np.arange(side, dtype=np.float32) * 2.0 / (2 * side))
    rows = np.zeros((8, half), np.float32)
    rows[0, :time] = ft
    rows[1, time : time + side] = fs
    rows[2, time + side :] = fs
    return np.repeat(rows, 2, axis=1)


def kernel(
    cfg,
    q_ref, k_ref, v_ref, pos_ref, fr_ref, qg_ref, kg_ref, ck_ref, cv_ref, cg_ref, cot_ref,
    so_ref, io_ref, gk_ref, gv_ref,
    Q, K, V, S, O, ORF, ORB, X1s, X1, X2, ST, MS, MR, LS, LR, G1s, G1, G2s, G2, G3, G4, qp,
    loc_sem, gs_sem, gr_sem, os_sem, or_sem, xs_sem, xr_sem,
):
    E, R, YH, N, T, W, H = cfg
    W2 = W * E
    scale = D ** -0.5
    e = lax.axis_index("enc")
    row = lax.axis_index("row")
    col = lax.axis_index("col")
    z = col // YH
    y = (col % YH) * R + row
    c = e % 2
    a = y * (1 - c) + z * c
    b = z * (1 - c) + y * c
    FW = N // 2
    BW = N - 1 - FW

    def dev(e_, y_, z_):
        return (e_, y_ % R, z_ * YH + y_ // R)

    def e_dev(d):
        return dev((e + d) % E, y, z)

    def y_dev(d):
        return dev(e, (y + d) % N, z)

    def z_dev(d):
        return dev(e, y, (z + d) % N)

    def a_dev(p):
        return dev(e, (1 - c) * p + c * y, (1 - c) * z + c * p)

    def b_dev(p):
        return dev(e, (1 - c) * y + c * p, (1 - c) * p + c * z)

    def row_dev(d):
        return (e, (row + d) % R, col)

    def remote(src, dst, ssem, rsem, device):
        return pltpu.make_async_remote_copy(
            src_ref=src, dst_ref=dst, send_sem=ssem, recv_sem=rsem,
            device_id=device, device_id_type=MESH,
        )

    bar = pltpu.get_barrier_semaphore()
    peers = [e_dev(d) for d in range(1, E)]
    peers += [y_dev(d) for d in range(1, N)] + [z_dev(d) for d in range(1, N)]
    for p in peers:
        pl.semaphore_signal(bar, inc=1, device_id=p, device_id_type=MESH)

    BAR = len(peers)

    def fwd_pos(p, s):
        return (p + (1 - 2 * c) * s + 2 * N) % N

    def ring(i, buf, p, who, h, fwd, s):
        sg = 1 if fwd else -1
        rows = pl.ds(pl.multiple_of(fwd_pos(p, -sg * s) * T, T), T)
        sl = buf.at[:, rows, :] if h is None else buf.at[h, rows, :]
        k_ = s if fwd else FW + s
        g = 0 if h is None else h
        return remote(
            sl, sl, gs_sem.at[i, g, k_], gr_sem.at[i, g, k_], who(fwd_pos(p, sg))
        )

    rings = {"q": (0, Q, a, a_dev), "k": (1, K, b, b_dev), "v": (2, V, b, b_dev)}

    def ring_start(t, h, s):
        if s < FW:
            ring(*rings[t], h, True, s).start()
        if s < BW:
            ring(*rings[t], h, False, s).start()

    def ring_recv(t, h, s):
        if s < FW:
            ring(*rings[t], h, True, s).wait_recv()
        if s < BW:
            ring(*rings[t], h, False, s).wait_recv()

    def ring_sent(t, h):
        for s in range(FW):
            ring(*rings[t], h, True, s).wait_send()
        for s in range(BW):
            ring(*rings[t], h, False, s).wait_send()

    def ring_next(t, h, s):
        if s >= FW:
            return
        ring_recv(t, h, s - 1)
        ring_start(t, h, s)

    a0 = pl.multiple_of(a * T, T)
    b0 = pl.multiple_of(b * T, T)
    for h in range(H):
        pltpu.make_async_copy(
            v_ref.at[:, pl.ds(h * D, D)], V.at[h, pl.ds(b0, T), :], loc_sem.at[h]
        ).start()

    eye = lax.broadcasted_iota(jnp.int32, (T, T), 0) == lax.broadcasted_iota(jnp.int32, (T, T), 1)

    def to_row(colv):
        return jnp.sum(jnp.where(eye, jnp.broadcast_to(colv, (T, T)), 0.0), axis=0, keepdims=True)

    def to_col(rowv):
        return jnp.sum(jnp.where(eye, jnp.broadcast_to(rowv, (T, T)), 0.0), axis=1, keepdims=True)

    qw = q_ref[...].astype(f32)
    kw = k_ref[...].astype(f32)
    srow_q = to_row(jnp.sum(qw * qw, axis=1, keepdims=True))
    srow_k = to_row(jnp.sum(kw * kw, axis=1, keepdims=True))
    sub8 = lax.broadcasted_iota(jnp.int32, (8, T), 0)
    ST[e] = jnp.where(sub8 < 4, jnp.broadcast_to(srow_q, (8, T)), jnp.broadcast_to(srow_k, (8, T)))

    def xch(i, d, src, dst, device):
        return remote(src, dst, xs_sem.at[i, d], xr_sem.at[i, d], device)

    def st_x(d):
        return xch(0, d, ST.at[e], ST.at[e], e_dev(d))

    pl.semaphore_wait(bar, BAR)
    for d in range(1, E):
        st_x(d).start()

    for h in range(H):
        pltpu.make_async_copy(
            v_ref.at[:, pl.ds(h * D, D)], V.at[h, pl.ds(b0, T), :], loc_sem.at[h]
        ).wait()
    ring_start("v", None, 0)

    ckw = ck_ref[...].astype(f32)
    crecip = lax.rsqrt(jnp.mean(ckw * ckw, axis=1, keepdims=True) + EPS)
    cn = (ckw * crecip * cg_ref[...].reshape(1, W2)).astype(bf16).astype(f32)
    cvw = cv_ref[...].astype(f32)
    for j in range(E):
        X1s[j, 0:4, :] = cn[:, j * W : (j + 1) * W]
        X1s[j, 4:8, :] = cvw[:, j * W : (j + 1) * W]

    def x1_x(d):
        return xch(1, d, X1s.at[(e + d) % E], X1.at[e], e_dev(d))

    for d in range(1, E):
        x1_x(d).start()
    X1[e] = X1s[e]

    coords = pos_ref[...].astype(f32)
    ang = (
        to_col(coords[0:1, :]) * fr_ref[0:1, :]
        + to_col(coords[1:2, :]) * fr_ref[1:2, :]
        + to_col(coords[2:3, :]) * fr_ref[2:3, :]
    )
    lane = lax.broadcasted_iota(jnp.int32, (T, D), 1)
    even = lane % 2 == 0
    cosv = jnp.cos(ang)
    sinv = jnp.sin(ang)
    sinv = jnp.where(even, -sinv, sinv)

    ring_next("v", None, 1)
    for d in range(1, E):
        st_x(d).wait_recv()
    tot = ST[0]
    for j in range(1, E):
        tot = tot + ST[j]
    qn = qw * lax.rsqrt(to_col(tot[0:1, :]) / W2 + EPS) * qg_ref[...].reshape(1, W)
    kn = kw * lax.rsqrt(to_col(tot[4:5, :]) / W2 + EPS) * kg_ref[...].reshape(1, W)
    qp[...] = qn.astype(bf16)

    def turn(x):
        swapped = jnp.where(even, pltpu.roll(x, D - 1, 1), pltpu.roll(x, 1, 1))
        return (x * cosv + swapped * sinv).astype(bf16)

    for h in range(H):
        Q[h, pl.ds(a0, T), :] = turn(qn[:, h * D : (h + 1) * D])
        ring_start("q", h, 0)
        K[h, pl.ds(b0, T), :] = turn(kn[:, h * D : (h + 1) * D])
        ring_start("k", h, 0)

    for d in range(1, E):
        x1_x(d).wait_recv()
    X2[row] = X1[...].reshape(E * 8, W).astype(bf16)

    sig = 1 - 2 * c
    offs = {1: [], 2: [1], 4: [1, -1, 2 * sig]}[R]

    def x2_x(d):
        return xch(2, d, X2.at[row], X2.at[row], y_dev(offs[d] + N))

    for d in range(len(offs)):
        x2_x(d).start()
    for s in range(1, FW):
        for h in range(H):
            ring_next("q", h, s)
            ring_next("k", h, s)
    for d in range(len(offs)):
        x2_x(d).wait_recv()

    C2 = R * E * 8
    xall = X2[...].reshape(C2, W)
    xval = pltpu.roll(xall.astype(f32), C2 - 4, 0).astype(bf16)
    is_key_l = lax.broadcasted_iota(jnp.int32, (T, C2), 1) % 8 < 4
    is_key_s = lax.broadcasted_iota(jnp.int32, (C2, D), 0) % 8 < 4

    def image_head(h):
        hs = slice(h * D, (h + 1) * D)
        qh = qp[:, hs]
        th = cot_ref[:, hs]
        sc = dot(qh, xall[:, hs], NT) * scale
        sc = jnp.where(is_key_l, sc, NEG)
        w = jnp.exp(sc - jnp.max(sc, axis=1, keepdims=True))
        pr = w / jnp.sum(w, axis=1, keepdims=True)
        plo = pr.astype(bf16)
        io_ref[:, hs] = dot(plo, xval[:, hs], NN).astype(bf16)
        gv = dot(plo, th, TN)
        gp = dot(th, xval[:, hs], NT)
        inner = jnp.sum(pr * gp, axis=1, keepdims=True)
        gsc = (pr * (gp - inner)).astype(bf16)
        gk = dot(gsc, qh, TN) * scale
        both = jnp.where(is_key_s, gk, pltpu.roll(gv, 4, 0))
        for r in range(R):
            for j in range(E):
                lo = (r * E + j) * 8
                G1s[j, r, :, hs] = both[lo : lo + 8, :]

    for h in range(H):
        image_head(h)
    ring_next("v", None, 2)

    def g1_x(d):
        j = (z + d) % N
        return xch(3, d, G1s.at[j], G1.at[z], z_dev(d))

    for d in range(1, N):
        g1_x(d).start()
    G1[z] = G1s[z]

    def pass1(h):
        def body(i, carry):
            rows = pl.ds(pl.multiple_of(i * 2 * T, 2 * T), 2 * T)
            s = dot(Q[h, rows, :], K[h], NT)
            S[h, rows, :] = s
            m = jnp.max(s, axis=1, keepdims=True)
            MS[h, pl.ds(2 * i, 1), :] = to_row(m[:T])
            MS[h, pl.ds(2 * i + 1, 1), :] = to_row(m[T:])
            return carry

        lax.fori_loop(0, N // 2, body, 0)

    def m_x(h, d):
        return xch(6 + h, d, MS.at[h], MR.at[h, a], a_dev((a + d) % N))

    def send_max(h):
        for d in range(1, N):
            m_x(h, d).start()
        MR[h, a] = MS[h]

    for h in range(H):
        ring_recv("q", h, FW - 1)
        ring_recv("k", h, FW - 1)
        pass1(h)
        send_max(h)
        if h == 0:
            ring_next("v", None, 3)

    def of(h, s):
        t = fwd_pos(a, FW - s)
        return remote(
            O.at[h, t], ORF.at[h, s], os_sem.at[h, s], or_sem.at[h, s], a_dev(fwd_pos(a, 1))
        ), t

    def ob(h, s):
        t = fwd_pos(a, s - BW)
        return remote(
            O.at[h, t], ORB.at[h, s], os_sem.at[h, FW + s], or_sem.at[h, FW + s],
            a_dev(fwd_pos(a, -1)),
        ), t

    def o_step(h, s):
        if s < FW:
            of(h, s - 1)[0].wait_recv()
            cp, t = of(h, s)
            O[h, t] = O[h, t] + ORF[h, s - 1]
            cp.start()
        if s < BW:
            ob(h, s - 1)[0].wait_recv()
            cp, t = ob(h, s)
            O[h, t] = O[h, t] + ORB[h, s - 1]
            cp.start()

    def pass2(h):
        for d in range(1, N):
            m_x(h, d).wait_recv()
        gm = MR[h, 0]
        for j in range(1, N):
            gm = jnp.maximum(gm, MR[h, j])
        MS[H] = gm

        def weights(k_):
            i = fwd_pos(a, (2 * (k_ % 2) - 1) * (FW - (k_ + 1) // 2))
            rows = pl.ds(pl.multiple_of(i * T, T), T)
            mc = to_col(MS[H, pl.ds(i, 1), :])
            w = jnp.exp2((S[h, rows, :] - mc) * (scale * math.log2(math.e)))
            LS[i, h : h + 1, :] = to_row(jnp.sum(w, axis=1, keepdims=True))
            return i, w.astype(bf16)

        def body(k_, carry):
            i, w1 = weights(2 * k_)
            j, w2 = weights(2 * k_ + 1)
            o = dot(jnp.concatenate([w1, w2], axis=0), V[h], NN)
            O[h, i] = o[:T]
            O[h, j] = o[T:]
            return carry

        body(0, 0)
        of(h, 0)[0].start()
        body(1, 0)
        ob(h, 0)[0].start()
        lax.fori_loop(2, N // 2, body, 0)

    def l_x(d):
        p = (a + d) % N
        return xch(5, d, LS.at[p], LR.at[a], a_dev(p))

    def g2_x(d):
        return xch(4, d, G2s.at[(y + d) % N % R], G2.at[y], y_dev(d))

    def g3_x(d):
        i = 6 + H
        return remote(
            G3.at[0], G4.at[e], xs_sem.at[i, d], xr_sem.at[i, e], dev(z, y, (z + d) % N)
        )

    def g3_from(d):
        i, j = 6 + H, (e + d) % E
        return remote(G3.at[0], G4.at[j], xs_sem.at[i, d], xr_sem.at[i, j], dev(j, y, e))

    ring_recv("v", None, FW - 1)
    for h in range(H):
        pass2(h)
        for j in range(h, -1, -1):
            o_step(j, h - j + 1)
        if h == 0:
            for d in range(1, N):
                g1_x(d).wait_recv()
            g = G1[0]
            for j in range(1, N):
                g = g + G1[j]
            G2s[...] = g
            for d in range(1, N):
                g2_x(d).start()
            G2[y] = G2s[row]
    for d in range(1, N):
        l_x(d).start()
    LR[a] = LS[a]

    for d in range(1, N):
        g2_x(d).wait_recv()
    g = G2[0]
    for j in range(1, N):
        g = g + G2[j]
    G3[0] = g

    @pl.when(e != z)
    def _():
        g3_x(0).start()

    @pl.when(e == z)
    def _():
        G4[e] = g

    for d in range(1, N):
        g3_x(d).start()

    lt = None
    for k_ in range(H, H + FW):
        for j in range(H - 1, -1, -1):
            s_ = k_ - j
            if 1 <= s_ < FW and s_ >= H - j + 1 - 0:
                o_step(j, s_)

    for d in range(1, N):
        l_x(d).wait_recv()
    lt = LR[0]
    for j in range(1, N):
        lt = lt + LR[j]
    for h in range(H):
        of(h, FW - 1)[0].wait_recv()
        ob(h, BW - 1)[0].wait_recv()
        acc = O[h, a] + ORF[h, FW - 1] + ORB[h, BW - 1]
        so_ref[:, h * D : (h + 1) * D] = (acc / to_col(lt[h : h + 1, :])).astype(bf16)

    @pl.when(e != z)
    def _():
        g3_from(0).wait_recv()

    for d in range(1, E):
        g3_from(d).wait_recv()
    for j in range(E):
        js = slice(j * W, (j + 1) * W)
        gv_ref[:, js] = G4[j, 4:8, :]
        gk_ref[:, js] = G4[j, 0:4, :]
    sg = cg_ref[...].reshape(1, W2) * gk_ref[...]
    gk_ref[...] = crecip * sg - ckw * (crecip * crecip * crecip) * jnp.mean(
        ckw * sg, axis=1, keepdims=True
    )

    for h in range(H):
        ring_sent("q", h)
        ring_sent("k", h)
        for s in range(FW):
            of(h, s)[0].wait_send()
        for s in range(BW):
            ob(h, s)[0].wait_send()
    ring_sent("v", None)
    for d in range(1, E):
        st_x(d).wait_send()
        x1_x(d).wait_send()
    for d in range(len(offs)):
        x2_x(d).wait_send()

    @pl.when(e != z)
    def _():
        g3_x(0).wait_send()

    for d in range(1, N):
        g1_x(d).wait_send()
        g2_x(d).wait_send()
        g3_x(d).wait_send()
        l_x(d).wait_send()
        for h in range(H):
            m_x(h, d).wait_send()


def copy_kernel(*refs):
    for src, dst in zip(refs[:4], refs[4:]):
        dst[...] = src[...]


def per_device(mesh_shape, q, k, v, pos, qg, kg, ck, cv, cg, cot):
    E, R, CL = mesh_shape
    T, W = q.shape
    H = W // D
    N = int(math.isqrt(R * CL))
    YH = N // R
    cfg = (E, R, YH, N, T, W, H)
    vm = pl.BlockSpec(memory_space=pltpu.VMEM)
    dma = pltpu.SemaphoreType.DMA
    out_shape = (
        jax.ShapeDtypeStruct((T, W), bf16),
        jax.ShapeDtypeStruct((T, W), bf16),
        jax.ShapeDtypeStruct(ck.shape, f32),
        jax.ShapeDtypeStruct(ck.shape, f32),
    )
    MX = max(E, N)
    scratch = [
        pltpu.VMEM((H, N * T, D), bf16),
        pltpu.VMEM((H, N * T, D), bf16),
        pltpu.VMEM((H, N * T, D), bf16),
        pltpu.VMEM((H, N * T, N * T), f32),
        pltpu.VMEM((H, N, T, D), f32),
        pltpu.VMEM((H, N // 2, T, D), f32),
        pltpu.VMEM((H, N // 2, T, D), f32),
        pltpu.VMEM((E, 8, W), f32),
        pltpu.VMEM((E, 8, W), f32),
        pltpu.VMEM((R, E * 8, W), bf16),
        pltpu.VMEM((E, 8, T), f32),
        pltpu.VMEM((H + 1, N, T), f32),
        pltpu.VMEM((H, N, N, T), f32),
        pltpu.VMEM((N, 8, T), f32),
        pltpu.VMEM((N, 8, T), f32),
        pltpu.VMEM((N, R, 8, W), f32),
        pltpu.VMEM((N, R, 8, W), f32),
        pltpu.VMEM((R, 8, W), f32),
        pltpu.VMEM((N, 8, W), f32),
        pltpu.VMEM((N, 8, W), f32),
        pltpu.VMEM((E, 8, W), f32),
        pltpu.VMEM((T, W), bf16),
        dma((H,)),
        dma((3, H, N)),
        dma((3, H, N)),
        dma((H, N)),
        dma((H, N)),
        dma((8 + H, MX)),
        dma((8 + H, MX)),
    ]
    res = pl.pallas_call(
        functools.partial(kernel, cfg),
        out_shape=out_shape,
        in_specs=[vm] * 11,
        out_specs=(vm,) * 4,
        scratch_shapes=scratch,
        compiler_params=pltpu.CompilerParams(
            collective_id=0, has_side_effects=True, vmem_limit_bytes=56 * 2**20
        ),
    )(q, k, v, pos.T, jnp.asarray(freq_rows()), qg, kg, ck, cv, cg, cot)
    return pl.pallas_call(
        copy_kernel, out_shape=out_shape, in_specs=[vm] * 4, out_specs=(vm,) * 4
    )(*res)


def solution(mesh):
    shape = (mesh.shape["enc"], mesh.shape["row"], mesh.shape["col"])
    tok = P(("row", "col"), "enc")
    ctx = P(("enc", "row"), None)
    return jax.shard_map(
        functools.partial(per_device, shape),
        mesh=mesh,
        in_specs=(tok, tok, tok, P(("row", "col"), None), P("enc"), P("enc"), ctx, ctx, P(), tok),
        out_specs=(tok, tok, ctx, ctx),
        check_vma=False,
    )
```

```python
import functools
import math
import jax
import jax.numpy as jnp
import numpy as np
from jax import lax
from jax.experimental import pallas as pl
from jax.experimental.pallas import tpu as pltpu
from jax.sharding import PartitionSpec as P

D = 128
EPS = 1e-06
MESH = pl.DeviceIdType.MESH
f32 = jnp.float32
bf16 = jnp.bfloat16
NEG = -1e30
NT = (((1,), (1,)), ((), ()))
NN = (((1,), (0,)), ((), ()))
TN = (((0,), (0,)), ((), ()))


def dot(a, b, dims):
    return lax.dot_general(a, b, dims, preferred_element_type=f32)


def freq_rows():
    half = D // 2
    side = D // 6
    time = half - 2 * side
    ft = 1.0 / 10000.0 ** (np.arange(time, dtype=np.float32) * 2.0 / (2 * time))
    fs = 1.0 / 10000.0 ** (np.arange(side, dtype=np.float32) * 2.0 / (2 * side))
    rows = np.zeros((8, half), np.float32)
    rows[0, :time] = ft
    rows[1, time : time + side] = fs
    rows[2, time + side :] = fs
    return np.repeat(rows, 2, axis=1)


def kernel(
    cfg,
    q_ref, k_ref, v_ref, pos_ref, fr_ref, qg_ref, kg_ref, ck_ref, cv_ref, cg_ref, cot_ref,
    so_ref, io_ref, gk_ref, gv_ref,
    Q, K, V, S, O, ORF, ORB, X1s, X1, X2, ST, MS, MR, LS, LR, G1s, G1, G2s, G2, G3, G4, qp,
    loc_sem, gs_sem, gr_sem, os_sem, or_sem, xs_sem, xr_sem,
):
    E, R, YH, N, T, W, H = cfg
    W2 = W * E
    scale = D ** -0.5
    e = lax.axis_index("enc")
    row = lax.axis_index("row")
    col = lax.axis_index("col")
    z = col // YH
    y = (col % YH) * R + row
    c = e % 2
    a = y * (1 - c) + z * c
    b = z * (1 - c) + y * c
    FW = N // 2
    BW = N - 1 - FW

    def dev(e_, y_, z_):
        return (e_, y_ % R, z_ * YH + y_ // R)

    def e_dev(d):
        return dev((e + d) % E, y, z)

    def y_dev(d):
        return dev(e, (y + d) % N, z)

    def z_dev(d):
        return dev(e, y, (z + d) % N)

    def a_dev(p):
        return dev(e, (1 - c) * p + c * y, (1 - c) * z + c * p)

    def b_dev(p):
        return dev(e, (1 - c) * y + c * p, (1 - c) * p + c * z)

    def row_dev(d):
        return (e, (row + d) % R, col)

    def remote(src, dst, ssem, rsem, device):
        return pltpu.make_async_remote_copy(
            src_ref=src, dst_ref=dst, send_sem=ssem, recv_sem=rsem,
            device_id=device, device_id_type=MESH,
        )

    bar = pltpu.get_barrier_semaphore()
    peers = [e_dev(d) for d in range(1, E)]
    peers += [y_dev(d) for d in range(1, N)] + [z_dev(d) for d in range(1, N)]
    for p in peers:
        pl.semaphore_signal(bar, inc=1, device_id=p, device_id_type=MESH)

    BAR = len(peers)

    def fwd_pos(p, s):
        return (p + (1 - 2 * c) * s + 2 * N) % N

    def ring(i, buf, p, who, h, fwd, s):
        sg = 1 if fwd else -1
        back, hop = sg * s, sg
        if h == 0 and fwd and s == FW - 1:
            back, hop = 0, FW
        rows = pl.ds(pl.multiple_of(fwd_pos(p, -back) * T, T), T)
        sl = buf.at[:, rows, :] if h is None else buf.at[h, rows, :]
        k_ = s if fwd else FW + s
        g = 0 if h is None else h
        return remote(
            sl, sl, gs_sem.at[i, g, k_], gr_sem.at[i, g, k_], who(fwd_pos(p, hop))
        )

    rings = {"q": (0, Q, a, a_dev), "k": (1, K, b, b_dev), "v": (2, V, b, b_dev)}

    def ring_start(t, h, s):
        if s < FW - 1 or (s == FW - 1 and h != 0):
            ring(*rings[t], h, True, s).start()
        if s < BW:
            ring(*rings[t], h, False, s).start()
        if s == 0 and h == 0:
            ring(*rings[t], h, True, FW - 1).start()

    def ring_recv(t, h, s):
        if s < FW:
            ring(*rings[t], h, True, s).wait_recv()
        if s < BW:
            ring(*rings[t], h, False, s).wait_recv()

    def ring_sent(t, h):
        for s in range(FW):
            ring(*rings[t], h, True, s).wait_send()
        for s in range(BW):
            ring(*rings[t], h, False, s).wait_send()

    def ring_next(t, h, s):
        if s >= FW:
            return
        ring_recv(t, h, s - 1)
        ring_start(t, h, s)

    a0 = pl.multiple_of(a * T, T)
    b0 = pl.multiple_of(b * T, T)
    for h in range(H):
        pltpu.make_async_copy(
            v_ref.at[:, pl.ds(h * D, D)], V.at[h, pl.ds(b0, T), :], loc_sem.at[h]
        ).start()

    eye = lax.broadcasted_iota(jnp.int32, (T, T), 0) == lax.broadcasted_iota(jnp.int32, (T, T), 1)

    def to_row(colv):
        return jnp.sum(jnp.where(eye, jnp.broadcast_to(colv, (T, T)), 0.0), axis=0, keepdims=True)

    def to_col(rowv):
        return jnp.sum(jnp.where(eye, jnp.broadcast_to(rowv, (T, T)), 0.0), axis=1, keepdims=True)

    qw = q_ref[...].astype(f32)
    kw = k_ref[...].astype(f32)
    srow_q = to_row(jnp.sum(qw * qw, axis=1, keepdims=True))
    srow_k = to_row(jnp.sum(kw * kw, axis=1, keepdims=True))
    sub8 = lax.broadcasted_iota(jnp.int32, (8, T), 0)
    ST[e] = jnp.where(sub8 < 4, jnp.broadcast_to(srow_q, (8, T)), jnp.broadcast_to(srow_k, (8, T)))

    def xch(i, d, src, dst, device):
        return remote(src, dst, xs_sem.at[i, d], xr_sem.at[i, d], device)

    def st_x(d):
        return xch(0, d, ST.at[e], ST.at[e], e_dev(d))

    pl.semaphore_wait(bar, BAR)
    for d in range(1, E):
        st_x(d).start()

    for h in range(H):
        pltpu.make_async_copy(
            v_ref.at[:, pl.ds(h * D, D)], V.at[h, pl.ds(b0, T), :], loc_sem.at[h]
        ).wait()
    ring_start("v", None, 0)

    ckw = ck_ref[...].astype(f32)
    crecip = lax.rsqrt(jnp.mean(ckw * ckw, axis=1, keepdims=True) + EPS)
    cn = (ckw * crecip * cg_ref[...].reshape(1, W2)).astype(bf16).astype(f32)
    cvw = cv_ref[...].astype(f32)
    for j in range(E):
        X1s[j, 0:4, :] = cn[:, j * W : (j + 1) * W]
        X1s[j, 4:8, :] = cvw[:, j * W : (j + 1) * W]

    def x1_x(d):
        return xch(1, d, X1s.at[(e + d) % E], X1.at[e], e_dev(d))

    for d in range(1, E):
        x1_x(d).start()
    X1[e] = X1s[e]

    coords = pos_ref[...].astype(f32)
    ang = (
        to_col(coords[0:1, :]) * fr_ref[0:1, :]
        + to_col(coords[1:2, :]) * fr_ref[1:2, :]
        + to_col(coords[2:3, :]) * fr_ref[2:3, :]
    )
    lane = lax.broadcasted_iota(jnp.int32, (T, D), 1)
    even = lane % 2 == 0
    cosv = jnp.cos(ang)
    sinv = jnp.sin(ang)
    sinv = jnp.where(even, -sinv, sinv)

    ring_next("v", None, 1)
    for d in range(1, E):
        st_x(d).wait_recv()
    tot = ST[0]
    for j in range(1, E):
        tot = tot + ST[j]
    qn = qw * lax.rsqrt(to_col(tot[0:1, :]) / W2 + EPS) * qg_ref[...].reshape(1, W)
    kn = kw * lax.rsqrt(to_col(tot[4:5, :]) / W2 + EPS) * kg_ref[...].reshape(1, W)
    qp[...] = qn.astype(bf16)

    def turn(x):
        swapped = jnp.where(even, pltpu.roll(x, D - 1, 1), pltpu.roll(x, 1, 1))
        return (x * cosv + swapped * sinv).astype(bf16)

    for h in range(H):
        Q[h, pl.ds(a0, T), :] = turn(qn[:, h * D : (h + 1) * D])
        ring_start("q", h, 0)
        K[h, pl.ds(b0, T), :] = turn(kn[:, h * D : (h + 1) * D])
        ring_start("k", h, 0)

    for d in range(1, E):
        x1_x(d).wait_recv()
    X2[row] = X1[...].reshape(E * 8, W).astype(bf16)

    sig = 1 - 2 * c
    offs = {1: [], 2: [1], 4: [1, -1, 2 * sig]}[R]

    def x2_x(d):
        return xch(2, d, X2.at[row], X2.at[row], y_dev(offs[d] + N))

    for d in range(len(offs)):
        x2_x(d).start()
    for s in range(1, FW):
        for h in range(H):
            ring_next("q", h, s)
            ring_next("k", h, s)
    for d in range(len(offs)):
        x2_x(d).wait_recv()

    C2 = R * E * 8
    xall = X2[...].reshape(C2, W)
    xval = pltpu.roll(xall.astype(f32), C2 - 4, 0).astype(bf16)
    is_key_l = lax.broadcasted_iota(jnp.int32, (T, C2), 1) % 8 < 4
    is_key_s = lax.broadcasted_iota(jnp.int32, (C2, D), 0) % 8 < 4

    def image_head(h):
        hs = slice(h * D, (h + 1) * D)
        qh = qp[:, hs]
        th = cot_ref[:, hs]
        sc = dot(qh, xall[:, hs], NT) * scale
        sc = jnp.where(is_key_l, sc, NEG)
        w = jnp.exp(sc - jnp.max(sc, axis=1, keepdims=True))
        pr = w / jnp.sum(w, axis=1, keepdims=True)
        plo = pr.astype(bf16)
        io_ref[:, hs] = dot(plo, xval[:, hs], NN).astype(bf16)
        gv = dot(plo, th, TN)
        gp = dot(th, xval[:, hs], NT)
        inner = jnp.sum(pr * gp, axis=1, keepdims=True)
        gsc = (pr * (gp - inner)).astype(bf16)
        gk = dot(gsc, qh, TN) * scale
        both = jnp.where(is_key_s, gk, pltpu.roll(gv, 4, 0))
        for j in range(E):
            rows = [both[(r * E + j) * 8 : (r * E + j + 1) * 8, :] for r in range(R)]
            G1s[j, :, hs] = jnp.concatenate(rows, axis=0).astype(bf16)

    for h in range(H):
        image_head(h)
    ring_next("v", None, 2)

    def g1_x(d):
        j = (z + d) % N
        return xch(3, d, G1s.at[j], G1.at[z], z_dev(d))

    for d in range(1, N):
        g1_x(d).start()
    G1[z] = G1s[z]

    def pass1(h):
        def body(i, carry):
            rows = pl.ds(pl.multiple_of(i * 2 * T, 2 * T), 2 * T)
            s = dot(Q[h, rows, :], K[h], NT)
            S[h, rows, :] = s
            m = jnp.max(s, axis=1, keepdims=True)
            MS[h, pl.ds(2 * i, 1), :] = to_row(m[:T])
            MS[h, pl.ds(2 * i + 1, 1), :] = to_row(m[T:])
            return carry

        lax.fori_loop(0, N // 2, body, 0)

    def m_x(h, d):
        return xch(6 + h, d, MS.at[h], MR.at[h, a], a_dev((a + d) % N))

    def send_max(h):
        for d in range(1, N):
            m_x(h, d).start()
        MR[h, a] = MS[h]

    for h in range(H):
        ring_recv("q", h, FW - 1)
        ring_recv("k", h, FW - 1)
        pass1(h)
        send_max(h)
        if h == 0:
            ring_next("v", None, 3)

    def of(h, s):
        t = fwd_pos(a, FW - s)
        return remote(
            O.at[h, t], ORF.at[h, s], os_sem.at[h, s], or_sem.at[h, s], a_dev(fwd_pos(a, 1))
        ), t

    def ob(h, s):
        t = fwd_pos(a, s - BW)
        return remote(
            O.at[h, t], ORB.at[h, s], os_sem.at[h, FW + s], or_sem.at[h, FW + s],
            a_dev(fwd_pos(a, -1)),
        ), t

    def o_step(h, s):
        if s < FW:
            of(h, s - 1)[0].wait_recv()
            cp, t = of(h, s)
            O[h, t] = O[h, t] + ORF[h, s - 1]
            cp.start()
        if s < BW:
            ob(h, s - 1)[0].wait_recv()
            cp, t = ob(h, s)
            O[h, t] = O[h, t] + ORB[h, s - 1]
            cp.start()

    def pass2(h):
        for d in range(1, N):
            m_x(h, d).wait_recv()
        gm = MR[h, 0]
        for j in range(1, N):
            gm = jnp.maximum(gm, MR[h, j])
        MS[H] = gm

        def weights(k_):
            i = fwd_pos(a, (2 * (k_ % 2) - 1) * (FW - (k_ + 1) // 2))
            rows = pl.ds(pl.multiple_of(i * T, T), T)
            mc = to_col(MS[H, pl.ds(i, 1), :])
            w = jnp.exp2((S[h, rows, :] - mc) * (scale * math.log2(math.e)))
            LS[i, h : h + 1, :] = to_row(jnp.sum(w, axis=1, keepdims=True))
            return i, w.astype(bf16)

        def body(k_, carry):
            i, w1 = weights(2 * k_)
            j, w2 = weights(2 * k_ + 1)
            o = dot(jnp.concatenate([w1, w2], axis=0), V[h], NN)
            O[h, i] = o[:T]
            O[h, j] = o[T:]
            return carry

        body(0, 0)
        of(h, 0)[0].start()
        body(1, 0)
        ob(h, 0)[0].start()
        lax.fori_loop(2, N // 2, body, 0)

    def l_x(d):
        p = (a + d) % N
        return xch(5, d, LS.at[p], LR.at[a], a_dev(p))

    def g2_x(d):
        return xch(4, d, G2s.at[(y + d) % N % R], G2.at[y], y_dev(d))

    def g3_x(d):
        i = 6 + H
        return remote(
            G3.at[0], G4.at[e], xs_sem.at[i, d], xr_sem.at[i, e], dev(z, y, (z + d) % N)
        )

    def g3_from(d):
        i, j = 6 + H, (e + d) % E
        return remote(G3.at[0], G4.at[j], xs_sem.at[i, d], xr_sem.at[i, j], dev(j, y, e))

    ring_recv("v", None, FW - 1)
    for h in range(H):
        pass2(h)
        for j in range(h, -1, -1):
            o_step(j, h - j + 1)
        if h == 0:
            for d in range(1, N):
                g1_x(d).wait_recv()
            g = G1[0].astype(f32)
            for j in range(1, N):
                g = g + G1[j].astype(f32)
            G2s[...] = g.reshape(R, 8, W)
            for d in range(1, N):
                g2_x(d).start()
            G2[y] = G2s[row]
    for d in range(1, N):
        l_x(d).start()
    LR[a] = LS[a]

    for d in range(1, N):
        g2_x(d).wait_recv()
    g = G2[0]
    for j in range(1, N):
        g = g + G2[j]
    G3[0] = g

    @pl.when(e != z)
    def _():
        g3_x(0).start()

    @pl.when(e == z)
    def _():
        G4[e] = g

    for d in range(1, N):
        g3_x(d).start()

    lt = None
    for k_ in range(H, H + FW):
        for j in range(H - 1, -1, -1):
            s_ = k_ - j
            if 1 <= s_ < FW and s_ >= H - j + 1 - 0:
                o_step(j, s_)

    for d in range(1, N):
        l_x(d).wait_recv()
    lt = LR[0]
    for j in range(1, N):
        lt = lt + LR[j]
    for h in range(H):
        of(h, FW - 1)[0].wait_recv()
        ob(h, BW - 1)[0].wait_recv()
        acc = O[h, a] + ORF[h, FW - 1] + ORB[h, BW - 1]
        so_ref[:, h * D : (h + 1) * D] = (acc / to_col(lt[h : h + 1, :])).astype(bf16)

    @pl.when(e != z)
    def _():
        g3_from(0).wait_recv()

    for d in range(1, E):
        g3_from(d).wait_recv()
    for j in range(E):
        js = slice(j * W, (j + 1) * W)
        gv_ref[:, js] = G4[j, 4:8, :]
        gk_ref[:, js] = G4[j, 0:4, :]
    sg = cg_ref[...].reshape(1, W2) * gk_ref[...]
    gk_ref[...] = crecip * sg - ckw * (crecip * crecip * crecip) * jnp.mean(
        ckw * sg, axis=1, keepdims=True
    )

    for h in range(H):
        ring_sent("q", h)
        ring_sent("k", h)
        for s in range(FW):
            of(h, s)[0].wait_send()
        for s in range(BW):
            ob(h, s)[0].wait_send()
    ring_sent("v", None)
    for d in range(1, E):
        st_x(d).wait_send()
        x1_x(d).wait_send()
    for d in range(len(offs)):
        x2_x(d).wait_send()

    @pl.when(e != z)
    def _():
        g3_x(0).wait_send()

    for d in range(1, N):
        g1_x(d).wait_send()
        g2_x(d).wait_send()
        g3_x(d).wait_send()
        l_x(d).wait_send()
        for h in range(H):
            m_x(h, d).wait_send()


def copy_kernel(*refs):
    for src, dst in zip(refs[:4], refs[4:]):
        dst[...] = src[...]


def per_device(mesh_shape, q, k, v, pos, qg, kg, ck, cv, cg, cot):
    E, R, CL = mesh_shape
    T, W = q.shape
    H = W // D
    N = int(math.isqrt(R * CL))
    YH = N // R
    cfg = (E, R, YH, N, T, W, H)
    vm = pl.BlockSpec(memory_space=pltpu.VMEM)
    dma = pltpu.SemaphoreType.DMA
    out_shape = (
        jax.ShapeDtypeStruct((T, W), bf16),
        jax.ShapeDtypeStruct((T, W), bf16),
        jax.ShapeDtypeStruct(ck.shape, f32),
        jax.ShapeDtypeStruct(ck.shape, f32),
    )
    MX = max(E, N)
    scratch = [
        pltpu.VMEM((H, N * T, D), bf16),
        pltpu.VMEM((H, N * T, D), bf16),
        pltpu.VMEM((H, N * T, D), bf16),
        pltpu.VMEM((H, N * T, N * T), f32),
        pltpu.VMEM((H, N, T, D), f32),
        pltpu.VMEM((H, N // 2, T, D), f32),
        pltpu.VMEM((H, N // 2, T, D), f32),
        pltpu.VMEM((E, 8, W), f32),
        pltpu.VMEM((E, 8, W), f32),
        pltpu.VMEM((R, E * 8, W), bf16),
        pltpu.VMEM((E, 8, T), f32),
        pltpu.VMEM((H + 1, N, T), f32),
        pltpu.VMEM((H, N, N, T), f32),
        pltpu.VMEM((N, 8, T), f32),
        pltpu.VMEM((N, 8, T), f32),
        pltpu.VMEM((N, R * 8, W), bf16),
        pltpu.VMEM((N, R * 8, W), bf16),
        pltpu.VMEM((R, 8, W), f32),
        pltpu.VMEM((N, 8, W), f32),
        pltpu.VMEM((N, 8, W), f32),
        pltpu.VMEM((E, 8, W), f32),
        pltpu.VMEM((T, W), bf16),
        dma((H,)),
        dma((3, H, N)),
        dma((3, H, N)),
        dma((H, N)),
        dma((H, N)),
        dma((8 + H, MX)),
        dma((8 + H, MX)),
    ]
    res = pl.pallas_call(
        functools.partial(kernel, cfg),
        out_shape=out_shape,
        in_specs=[vm] * 11,
        out_specs=(vm,) * 4,
        scratch_shapes=scratch,
        compiler_params=pltpu.CompilerParams(
            collective_id=0, has_side_effects=True, vmem_limit_bytes=56 * 2**20
        ),
    )(q, k, v, pos.T, jnp.asarray(freq_rows()), qg, kg, ck, cv, cg, cot)
    return pl.pallas_call(
        copy_kernel, out_shape=out_shape, in_specs=[vm] * 4, out_specs=(vm,) * 4
    )(*res)


def solution(mesh):
    shape = (mesh.shape["enc"], mesh.shape["row"], mesh.shape["col"])
    tok = P(("row", "col"), "enc")
    ctx = P(("enc", "row"), None)
    return jax.shard_map(
        functools.partial(per_device, shape),
        mesh=mesh,
        in_specs=(tok, tok, tok, P(("row", "col"), None), P("enc"), P("enc"), ctx, ctx, P(), tok),
        out_specs=(tok, tok, ctx, ctx),
        check_vma=False,
    )
```

```python
import functools
import math
import jax
import jax.numpy as jnp
import numpy as np
from jax import lax
from jax.experimental import pallas as pl
from jax.experimental.pallas import tpu as pltpu
from jax.sharding import PartitionSpec as P

D = 128
EPS = 1e-06
MESH = pl.DeviceIdType.MESH
f32 = jnp.float32
bf16 = jnp.bfloat16
NEG = -1e30
NT = (((1,), (1,)), ((), ()))
NN = (((1,), (0,)), ((), ()))
TN = (((0,), (0,)), ((), ()))


def dot(a, b, dims):
    return lax.dot_general(a, b, dims, preferred_element_type=f32)


def freq_rows():
    half = D // 2
    side = D // 6
    time = half - 2 * side
    ft = 1.0 / 10000.0 ** (np.arange(time, dtype=np.float32) * 2.0 / (2 * time))
    fs = 1.0 / 10000.0 ** (np.arange(side, dtype=np.float32) * 2.0 / (2 * side))
    rows = np.zeros((8, half), np.float32)
    rows[0, :time] = ft
    rows[1, time : time + side] = fs
    rows[2, time + side :] = fs
    return np.repeat(rows, 2, axis=1)


def kernel(
    cfg,
    q_ref, k_ref, v_ref, pos_ref, fr_ref, qg_ref, kg_ref, ck_ref, cv_ref, cg_ref, cot_ref,
    so_ref, io_ref, gk_ref, gv_ref,
    Q, K, V, S, O, ORF, ORB, X1s, X1, X2, ST, MS, MR, LS, LR, G1s, G1, G2s, G2, G3, G4, qp,
    loc_sem, gs_sem, gr_sem, os_sem, or_sem, xs_sem, xr_sem,
):
    E, R, YH, N, T, W, H = cfg
    W2 = W * E
    scale = D ** -0.5
    e = lax.axis_index("enc")
    row = lax.axis_index("row")
    col = lax.axis_index("col")
    z = col // YH
    y = (col % YH) * R + row
    c = e % 2
    a = y * (1 - c) + z * c
    b = z * (1 - c) + y * c
    FW = N // 2
    BW = N - 1 - FW

    def dev(e_, y_, z_):
        return (e_, y_ % R, z_ * YH + y_ // R)

    def e_dev(d):
        return dev((e + d) % E, y, z)

    def y_dev(d):
        return dev(e, (y + d) % N, z)

    def z_dev(d):
        return dev(e, y, (z + d) % N)

    def a_dev(p):
        return dev(e, (1 - c) * p + c * y, (1 - c) * z + c * p)

    def b_dev(p):
        return dev(e, (1 - c) * y + c * p, (1 - c) * p + c * z)

    def row_dev(d):
        return (e, (row + d) % R, col)

    def remote(src, dst, ssem, rsem, device):
        return pltpu.make_async_remote_copy(
            src_ref=src, dst_ref=dst, send_sem=ssem, recv_sem=rsem,
            device_id=device, device_id_type=MESH,
        )

    bar = pltpu.get_barrier_semaphore()
    peers = [e_dev(d) for d in range(1, E)]
    peers += [y_dev(d) for d in range(1, N)] + [z_dev(d) for d in range(1, N)]
    for p in peers:
        pl.semaphore_signal(bar, inc=1, device_id=p, device_id_type=MESH)

    BAR = len(peers)

    def fwd_pos(p, s):
        return (p + (1 - 2 * c) * s + 2 * N) % N

    def ring(i, buf, p, who, h, fwd, s):
        sg = 1 if fwd else -1
        back, hop = sg * s, sg
        if h == 0 and fwd and s == FW - 1:
            back, hop = 0, FW
        rows = pl.ds(pl.multiple_of(fwd_pos(p, -back) * T, T), T)
        sl = buf.at[:, rows, :] if h is None else buf.at[h, rows, :]
        k_ = s if fwd else FW + s
        g = 0 if h is None else h
        return remote(
            sl, sl, gs_sem.at[i, g, k_], gr_sem.at[i, g, k_], who(fwd_pos(p, hop))
        )

    rings = {"q": (0, Q, a, a_dev), "k": (1, K, b, b_dev), "v": (2, V, b, b_dev)}

    def ring_start(t, h, s):
        if s < FW - 1 or (s == FW - 1 and h != 0):
            ring(*rings[t], h, True, s).start()
        if s < BW:
            ring(*rings[t], h, False, s).start()
        if s == 0 and h == 0:
            ring(*rings[t], h, True, FW - 1).start()

    def ring_recv(t, h, s):
        if s < FW:
            ring(*rings[t], h, True, s).wait_recv()
        if s < BW:
            ring(*rings[t], h, False, s).wait_recv()

    def ring_sent(t, h):
        for s in range(FW):
            ring(*rings[t], h, True, s).wait_send()
        for s in range(BW):
            ring(*rings[t], h, False, s).wait_send()

    def ring_next(t, h, s):
        if s >= FW:
            return
        ring_recv(t, h, s - 1)
        ring_start(t, h, s)

    a0 = pl.multiple_of(a * T, T)
    b0 = pl.multiple_of(b * T, T)
    for h in range(H):
        pltpu.make_async_copy(
            v_ref.at[:, pl.ds(h * D, D)], V.at[h, pl.ds(b0, T), :], loc_sem.at[h]
        ).start()

    eye = lax.broadcasted_iota(jnp.int32, (T, T), 0) == lax.broadcasted_iota(jnp.int32, (T, T), 1)

    def to_row(colv):
        return jnp.sum(jnp.where(eye, jnp.broadcast_to(colv, (T, T)), 0.0), axis=0, keepdims=True)

    def to_col(rowv):
        return jnp.sum(jnp.where(eye, jnp.broadcast_to(rowv, (T, T)), 0.0), axis=1, keepdims=True)

    qw = q_ref[...].astype(f32)
    kw = k_ref[...].astype(f32)
    srow_q = to_row(jnp.sum(qw * qw, axis=1, keepdims=True))
    srow_k = to_row(jnp.sum(kw * kw, axis=1, keepdims=True))
    sub8 = lax.broadcasted_iota(jnp.int32, (8, T), 0)
    ST[e] = jnp.where(sub8 < 4, jnp.broadcast_to(srow_q, (8, T)), jnp.broadcast_to(srow_k, (8, T)))

    def xch(i, d, src, dst, device):
        return remote(src, dst, xs_sem.at[i, d], xr_sem.at[i, d], device)

    def st_x(d):
        return xch(0, d, ST.at[e], ST.at[e], e_dev(d))

    pl.semaphore_wait(bar, BAR)
    for d in range(1, E):
        st_x(d).start()

    for h in range(H):
        pltpu.make_async_copy(
            v_ref.at[:, pl.ds(h * D, D)], V.at[h, pl.ds(b0, T), :], loc_sem.at[h]
        ).wait()
    ring_start("v", None, 0)

    ckw = ck_ref[...].astype(f32)
    crecip = lax.rsqrt(jnp.mean(ckw * ckw, axis=1, keepdims=True) + EPS)
    cn = (ckw * crecip * cg_ref[...].reshape(1, W2)).astype(bf16).astype(f32)
    cvw = cv_ref[...].astype(f32)
    for j in range(E):
        X1s[j, 0:4, :] = cn[:, j * W : (j + 1) * W]
        X1s[j, 4:8, :] = cvw[:, j * W : (j + 1) * W]

    def x1_x(d):
        return xch(1, d, X1s.at[(e + d) % E], X1.at[e], e_dev(d))

    for d in range(1, E):
        x1_x(d).start()
    X1[e] = X1s[e]

    coords = pos_ref[...].astype(f32)
    ang = (
        to_col(coords[0:1, :]) * fr_ref[0:1, :]
        + to_col(coords[1:2, :]) * fr_ref[1:2, :]
        + to_col(coords[2:3, :]) * fr_ref[2:3, :]
    )
    lane = lax.broadcasted_iota(jnp.int32, (T, D), 1)
    even = lane % 2 == 0
    cosv = jnp.cos(ang)
    sinv = jnp.sin(ang)
    sinv = jnp.where(even, -sinv, sinv)

    ring_next("v", None, 1)
    for d in range(1, E):
        st_x(d).wait_recv()
    tot = ST[0]
    for j in range(1, E):
        tot = tot + ST[j]
    qn = qw * lax.rsqrt(to_col(tot[0:1, :]) / W2 + EPS) * qg_ref[...].reshape(1, W)
    kn = kw * lax.rsqrt(to_col(tot[4:5, :]) / W2 + EPS) * kg_ref[...].reshape(1, W)
    qp[...] = qn.astype(bf16)

    def turn(x):
        swapped = jnp.where(even, pltpu.roll(x, D - 1, 1), pltpu.roll(x, 1, 1))
        return (x * cosv + swapped * sinv).astype(bf16)

    for h in range(H):
        Q[h, pl.ds(a0, T), :] = turn(qn[:, h * D : (h + 1) * D])
        ring_start("q", h, 0)
        K[h, pl.ds(b0, T), :] = turn(kn[:, h * D : (h + 1) * D])
        ring_start("k", h, 0)

    for d in range(1, E):
        x1_x(d).wait_recv()
    X2[row] = X1[...].reshape(E * 8, W).astype(bf16)

    sig = 1 - 2 * c
    offs = {1: [], 2: [1], 4: [1, -1, 2 * sig]}[R]

    def x2_x(d):
        return xch(2, d, X2.at[row], X2.at[row], y_dev(offs[d] + N))

    for d in range(len(offs)):
        x2_x(d).start()
    for s in range(1, FW):
        for h in range(H):
            ring_next("q", h, s)
            ring_next("k", h, s)
    for d in range(len(offs)):
        x2_x(d).wait_recv()

    C2 = R * E * 8
    xall = X2[...].reshape(C2, W)
    xval = pltpu.roll(xall.astype(f32), C2 - 4, 0).astype(bf16)
    is_key_l = lax.broadcasted_iota(jnp.int32, (T, C2), 1) % 8 < 4
    is_key_s = lax.broadcasted_iota(jnp.int32, (C2, D), 0) % 8 < 4

    def image_head(h):
        hs = slice(h * D, (h + 1) * D)
        qh = qp[:, hs]
        th = cot_ref[:, hs]
        sc = dot(qh, xall[:, hs], NT) * scale
        sc = jnp.where(is_key_l, sc, NEG)
        w = jnp.exp(sc - jnp.max(sc, axis=1, keepdims=True))
        pr = w / jnp.sum(w, axis=1, keepdims=True)
        plo = pr.astype(bf16)
        io_ref[:, hs] = dot(plo, xval[:, hs], NN).astype(bf16)
        gv = dot(plo, th, TN)
        gp = dot(th, xval[:, hs], NT)
        inner = jnp.sum(pr * gp, axis=1, keepdims=True)
        gsc = (pr * (gp - inner)).astype(bf16)
        gk = dot(gsc, qh, TN) * scale
        both = jnp.where(is_key_s, gk, pltpu.roll(gv, 4, 0))
        for r in range(R):
            for j in range(E):
                lo = (r * E + j) * 8
                G1s[j, r, :, hs] = both[lo : lo + 8, :]

    for h in range(H):
        image_head(h)
    ring_next("v", None, 2)

    def g1_x(d):
        j = (z + d) % N
        return xch(3, d, G1s.at[j], G1.at[z], z_dev(d))

    for d in range(1, N):
        g1_x(d).start()
    G1[z] = G1s[z]

    def pass1(h):
        def body(i, carry):
            rows = pl.ds(pl.multiple_of(i * 2 * T, 2 * T), 2 * T)
            s = dot(Q[h, rows, :], K[h], NT)
            S[h, rows, :] = s
            m = jnp.max(s, axis=1, keepdims=True)
            MS[h, pl.ds(2 * i, 1), :] = to_row(m[:T])
            MS[h, pl.ds(2 * i + 1, 1), :] = to_row(m[T:])
            return carry

        lax.fori_loop(0, N // 2, body, 0)

    def m_x(h, d):
        return xch(6 + h, d, MS.at[h], MR.at[h, a], a_dev((a + d) % N))

    def send_max(h):
        for d in range(1, N):
            m_x(h, d).start()
        MR[h, a] = MS[h]

    for h in range(H):
        ring_recv("q", h, FW - 1)
        ring_recv("k", h, FW - 1)
        pass1(h)
        send_max(h)
        if h == 0:
            ring_next("v", None, 3)

    def of(h, s):
        t = fwd_pos(a, FW - s)
        return remote(
            O.at[h, t], ORF.at[h, s], os_sem.at[h, s], or_sem.at[h, s], a_dev(fwd_pos(a, 1))
        ), t

    def ob(h, s):
        t = fwd_pos(a, s - BW)
        return remote(
            O.at[h, t], ORB.at[h, s], os_sem.at[h, FW + s], or_sem.at[h, FW + s],
            a_dev(fwd_pos(a, -1)),
        ), t

    def o_step(h, s):
        if s < FW:
            of(h, s - 1)[0].wait_recv()
            cp, t = of(h, s)
            O[h, t] = O[h, t] + ORF[h, s - 1]
            cp.start()
        if s < BW:
            ob(h, s - 1)[0].wait_recv()
            cp, t = ob(h, s)
            O[h, t] = O[h, t] + ORB[h, s - 1]
            cp.start()

    def pass2(h):
        for d in range(1, N):
            m_x(h, d).wait_recv()
        gm = MR[h, 0]
        for j in range(1, N):
            gm = jnp.maximum(gm, MR[h, j])
        MS[H] = gm

        def weights(k_):
            i = fwd_pos(a, (2 * (k_ % 2) - 1) * (FW - (k_ + 1) // 2))
            rows = pl.ds(pl.multiple_of(i * T, T), T)
            mc = to_col(MS[H, pl.ds(i, 1), :])
            w = jnp.exp2((S[h, rows, :] - mc) * (scale * math.log2(math.e)))
            LS[i, h : h + 1, :] = to_row(jnp.sum(w, axis=1, keepdims=True))
            return i, w.astype(bf16)

        def body(k_, carry):
            i, w1 = weights(2 * k_)
            j, w2 = weights(2 * k_ + 1)
            o = dot(jnp.concatenate([w1, w2], axis=0), V[h], NN)
            O[h, i] = o[:T]
            O[h, j] = o[T:]
            return carry

        body(0, 0)
        of(h, 0)[0].start()
        body(1, 0)
        ob(h, 0)[0].start()
        lax.fori_loop(2, N // 2, body, 0)

    def l_x(d):
        p = (a + d) % N
        return xch(5, d, LS.at[p], LR.at[a], a_dev(p))

    def g2_x(d):
        return xch(4, d, G2s.at[(y + d) % N % R], G2.at[y], y_dev(d))

    def g3_x(d):
        i = 6 + H
        return remote(
            G3.at[0], G4.at[e], xs_sem.at[i, d], xr_sem.at[i, e], dev(z, y, (z + d) % N)
        )

    def g3_from(d):
        i, j = 6 + H, (e + d) % E
        return remote(G3.at[0], G4.at[j], xs_sem.at[i, d], xr_sem.at[i, j], dev(j, y, e))

    ring_recv("v", None, FW - 1)
    for h in range(H):
        pass2(h)
        for j in range(h, -1, -1):
            o_step(j, h - j + 1)
        if h == max(H - 2, 0):
            for d in range(1, N):
                g1_x(d).wait_recv()
            g = G1[0]
            for j in range(1, N):
                g = g + G1[j]
            G2s[...] = g
            for d in range(1, N):
                g2_x(d).start()
            G2[y] = G2s[row]
    for d in range(1, N):
        l_x(d).start()
    LR[a] = LS[a]

    for d in range(1, N):
        g2_x(d).wait_recv()
    g = G2[0]
    for j in range(1, N):
        g = g + G2[j]
    G3[0] = g

    @pl.when(e != z)
    def _():
        g3_x(0).start()

    @pl.when(e == z)
    def _():
        G4[e] = g

    for d in range(1, N):
        g3_x(d).start()

    lt = None
    for k_ in range(H, H + FW):
        for j in range(H - 1, -1, -1):
            s_ = k_ - j
            if 1 <= s_ < FW and s_ >= H - j + 1 - 0:
                o_step(j, s_)

    for d in range(1, N):
        l_x(d).wait_recv()
    lt = LR[0]
    for j in range(1, N):
        lt = lt + LR[j]
    for h in range(H):
        of(h, FW - 1)[0].wait_recv()
        ob(h, BW - 1)[0].wait_recv()
        acc = O[h, a] + ORF[h, FW - 1] + ORB[h, BW - 1]
        so_ref[:, h * D : (h + 1) * D] = (acc / to_col(lt[h : h + 1, :])).astype(bf16)

    @pl.when(e != z)
    def _():
        g3_from(0).wait_recv()

    for d in range(1, E):
        g3_from(d).wait_recv()
    for j in range(E):
        js = slice(j * W, (j + 1) * W)
        gv_ref[:, js] = G4[j, 4:8, :]
        gk_ref[:, js] = G4[j, 0:4, :]
    sg = cg_ref[...].reshape(1, W2) * gk_ref[...]
    gk_ref[...] = crecip * sg - ckw * (crecip * crecip * crecip) * jnp.mean(
        ckw * sg, axis=1, keepdims=True
    )

    for h in range(H):
        ring_sent("q", h)
        ring_sent("k", h)
        for s in range(FW):
            of(h, s)[0].wait_send()
        for s in range(BW):
            ob(h, s)[0].wait_send()
    ring_sent("v", None)
    for d in range(1, E):
        st_x(d).wait_send()
        x1_x(d).wait_send()
    for d in range(len(offs)):
        x2_x(d).wait_send()

    @pl.when(e != z)
    def _():
        g3_x(0).wait_send()

    for d in range(1, N):
        g1_x(d).wait_send()
        g2_x(d).wait_send()
        g3_x(d).wait_send()
        l_x(d).wait_send()
        for h in range(H):
            m_x(h, d).wait_send()


def copy_kernel(*refs):
    for src, dst in zip(refs[:4], refs[4:]):
        dst[...] = src[...]


def per_device(mesh_shape, q, k, v, pos, qg, kg, ck, cv, cg, cot):
    E, R, CL = mesh_shape
    T, W = q.shape
    H = W // D
    N = int(math.isqrt(R * CL))
    YH = N // R
    cfg = (E, R, YH, N, T, W, H)
    vm = pl.BlockSpec(memory_space=pltpu.VMEM)
    dma = pltpu.SemaphoreType.DMA
    out_shape = (
        jax.ShapeDtypeStruct((T, W), bf16),
        jax.ShapeDtypeStruct((T, W), bf16),
        jax.ShapeDtypeStruct(ck.shape, f32),
        jax.ShapeDtypeStruct(ck.shape, f32),
    )
    MX = max(E, N)
    scratch = [
        pltpu.VMEM((H, N * T, D), bf16),
        pltpu.VMEM((H, N * T, D), bf16),
        pltpu.VMEM((H, N * T, D), bf16),
        pltpu.VMEM((H, N * T, N * T), f32),
        pltpu.VMEM((H, N, T, D), f32),
        pltpu.VMEM((H, N // 2, T, D), f32),
        pltpu.VMEM((H, N // 2, T, D), f32),
        pltpu.VMEM((E, 8, W), f32),
        pltpu.VMEM((E, 8, W), f32),
        pltpu.VMEM((R, E * 8, W), bf16),
        pltpu.VMEM((E, 8, T), f32),
        pltpu.VMEM((H + 1, N, T), f32),
        pltpu.VMEM((H, N, N, T), f32),
        pltpu.VMEM((N, 8, T), f32),
        pltpu.VMEM((N, 8, T), f32),
        pltpu.VMEM((N, R, 8, W), f32),
        pltpu.VMEM((N, R, 8, W), f32),
        pltpu.VMEM((R, 8, W), f32),
        pltpu.VMEM((N, 8, W), f32),
        pltpu.VMEM((N, 8, W), f32),
        pltpu.VMEM((E, 8, W), f32),
        pltpu.VMEM((T, W), bf16),
        dma((H,)),
        dma((3, H, N)),
        dma((3, H, N)),
        dma((H, N)),
        dma((H, N)),
        dma((8 + H, MX)),
        dma((8 + H, MX)),
    ]
    res = pl.pallas_call(
        functools.partial(kernel, cfg),
        out_shape=out_shape,
        in_specs=[vm] * 11,
        out_specs=(vm,) * 4,
        scratch_shapes=scratch,
        compiler_params=pltpu.CompilerParams(
            collective_id=0, has_side_effects=True, vmem_limit_bytes=56 * 2**20
        ),
    )(q, k, v, pos.T, jnp.asarray(freq_rows()), qg, kg, ck, cv, cg, cot)
    return pl.pallas_call(
        copy_kernel, out_shape=out_shape, in_specs=[vm] * 4, out_specs=(vm,) * 4
    )(*res)


def solution(mesh):
    shape = (mesh.shape["enc"], mesh.shape["row"], mesh.shape["col"])
    tok = P(("row", "col"), "enc")
    ctx = P(("enc", "row"), None)
    return jax.shard_map(
        functools.partial(per_device, shape),
        mesh=mesh,
        in_specs=(tok, tok, tok, P(("row", "col"), None), P("enc"), P("enc"), ctx, ctx, P(), tok),
        out_specs=(tok, tok, ctx, ctx),
        check_vma=False,
    )
```
